32 devices in a mesh: elem: 16 (over z, x, core), section: 2 (over y).
Axes of the slice: x: 2, y: 2, z: 4, core: 2. Of those that a mesh axis runs over, the one named last changes fastest.
Arguments:
- u_start: float32 [512, 320], P('elem'), may hold values from -6 to 6
- inverses: float32 [512, 320, 320], P('elem'), may hold values from -1 to 2
- neighbours: int32 [512, 5], P('elem'), may hold values from 0 to 511, as said below
- partners: int32 [512], replicated, may hold values from 0 to 511, as said below
Outputs:
- section_states: float32 [4, 512, 320], P('section', 'elem')
The draws below stay inside these ranges and needn't reach their ends.
Inputs may be any that keep to these rules, and one draw needn't show every extreme that they name: `neighbours`: every entry names an element on the same device as the row's element, or on the device just before or after it along elem, cyclically. The partners of the 32 elements of device d along elem lie on devices d + 4 and d + 5, cyclically, 16 on each.
All inputs are finite; a program needn't handle non-finite values.
Results may differ from the reference program's by a relative error of at most 0.0001.
Values sent between devices are 32-bit elements; how exact they have to be, the bound alone decides.
A program may use at most 64 MiB of HBM per device.

```python
import math
import jax
import jax.numpy as jnp
from jax import lax

NODE1 = 4
UNK = 320
SECTIONS = 4
NEWTON = 2
E_DEV = 32
NE = 512


def draw_inverses(key, part):
    key_diag, key_off = jax.random.split(jax.random.fold_in(key, 11))
    diagonal_vals = jax.random.uniform(key_diag, (NE, UNK), jnp.float32, 0.6, 1.0)
    off_diag = jax.random.normal(key_off, (NE, UNK, UNK), jnp.float32) * (0.3 / UNK ** 0.5)
    return off_diag + diagonal_vals[:, :, None] * jnp.eye(UNK, dtype=jnp.float32)[None]


def draw_neighbours(key, part):
    devices = NE // E_DEV
    key_shift, key_local = jax.random.split(jax.random.fold_in(key, 23))
    shift_rows = jax.random.randint(key_shift, (NE, 5), -1, 2)
    owner_dev = (jnp.arange(NE, dtype=jnp.int32) // E_DEV)[:, None]
    target_dev = (owner_dev + shift_rows + devices) % devices
    local_rows = jax.random.randint(key_local, (NE, 5), 0, E_DEV)
    return (target_dev * E_DEV + local_rows).astype(jnp.int32)


def draw_partners(key, part):
    devices = NE // E_DEV
    rotation = devices // 4
    key_order, key_local = jax.random.split(jax.random.fold_in(key, 37))

    def slot_order(dev_key):
        return jax.random.permutation(dev_key, E_DEV)
    orders = jax.vmap(slot_order)(jax.random.split(key_order, devices))
    upper = (orders >= E_DEV // 2).astype(jnp.int32)
    device_ids = jnp.arange(devices, dtype=jnp.int32)[:, None]
    target_dev = (device_ids + rotation + upper) % devices
    local_rows = jax.random.randint(key_local, (devices, E_DEV), 0, E_DEV)
    return (target_dev * E_DEV + local_rows).reshape(NE).astype(jnp.int32)


def steps_of(key, shape, pieces, least, top_value):
    def one(axis_at, parts):
        draws = jax.random.uniform(jax.random.fold_in(jax.random.fold_in(key, 6), axis_at), (parts,), jnp.float32, least / len(pieces), top_value / len(pieces))
        return jnp.repeat(jnp.exp(draws), shape[axis_at] // parts).reshape((-1,) + (1,) * (len(shape) - axis_at - 1))

    factor_of = one(*pieces[0])
    for cut in pieces[1:]:
        factor_of = factor_of * one(*cut)
    return factor_of


def noise(rng, dims, scale, reach, cuts=(), kind=jnp.bfloat16):
    gain = steps_of(rng, dims, cuts, -0.22, 0.18) if cuts else 1.0
    result = jax.random.normal(rng, dims, jnp.float32) * scale * gain
    return jnp.minimum(jnp.maximum(result, -reach), reach).astype(kind)


def setup_inputs(seed: int = 0) -> dict:
    keys = jax.random.split(jax.random.key(seed), 5)
    u_start = noise(keys[0], (NE, UNK), 1.0, 6.0, ((0, 16),), jnp.float32)
    inverses = draw_inverses(jax.random.fold_in(keys[4], 71), 0)
    neighbours = draw_neighbours(jax.random.fold_in(keys[4], 71), 0)
    partners = draw_partners(jax.random.fold_in(keys[4], 71), 0)
    return dict(u_start=u_start, inverses=inverses, neighbours=neighbours, partners=partners)


time_step = 0.03
dissipation = 2.0
enthalpy_factor = 3.5
radau_nodes = [0.08858795951270394, 0.4094668644407347, 0.787659461760847, 1.0]

def lobatto():
    node_count = NODE1
    if node_count == 4:
        inner_value = 1.0 / math.sqrt(5.0)
        lobatto_nodes = [-1.0, -inner_value, inner_value, 1.0]
    else:
        lobatto_nodes = [-1.0, 1.0]
    products = []
    for row in range(node_count):
        value = 1.0
        for other in range(node_count):
            if other != row:
                value = value * (lobatto_nodes[row] - lobatto_nodes[other])
        products.append(value)
    derivative = []
    for row in range(node_count):
        entries = []
        for column in range(node_count):
            if row == column:
                total = 0.0
                for other in range(node_count):
                    if other != row:
                        total = total + 1.0 / (lobatto_nodes[row] - lobatto_nodes[other])
                entries.append(2.0 * total)
            else:
                entries.append(2.0 * (products[row] / products[column]) / (lobatto_nodes[row] - lobatto_nodes[column]))
        derivative.append(entries)
    return (jnp.asarray(derivative, jnp.float32), float(node_count * (node_count - 1) / 2.0))

def radau_table():
    section_total = SECTIONS
    butcher = []
    columns = []
    for column in range(section_total):
        coeffs = [1.0]
        scale = 1.0
        for other in range(section_total):
            if other != column:
                shifted = [0.0] + coeffs
                for position in range(len(coeffs)):
                    shifted[position] = shifted[position] - radau_nodes[other] * coeffs[position]
                coeffs = shifted
                scale = scale * (radau_nodes[column] - radau_nodes[other])
        integral = [0.0] + [coeffs[position] / (position + 1.0) / scale for position in range(len(coeffs))]
        columns.append(integral)
    for row in range(section_total):
        entries = []
        for column in range(section_total):
            value = 0.0
            for coefficient in reversed(columns[column]):
                value = value * radau_nodes[row] + coefficient
            entries.append(value)
        butcher.append(entries)
    return butcher

def flux(left_state, right_state, direction):
    density = 0.5 * (left_state[:, :, 0] + right_state[:, :, 0])
    velocity = [0.5 * (left_state[:, :, 1 + comp] + right_state[:, :, 1 + comp]) for comp in range(3)]
    pressure = 0.5 * (left_state[:, :, 4] + right_state[:, :, 4])
    kinetic = 0.0
    for comp in range(3):
        kinetic = kinetic + 0.5 * (left_state[:, :, 1 + comp] ** 2 + right_state[:, :, 1 + comp] ** 2)
    normal_speed = velocity[direction]
    mass_flux = density * normal_speed
    components = [mass_flux]
    for comp in range(3):
        momentum = mass_flux * velocity[comp]
        if comp == direction:
            momentum = momentum + pressure
        components.append(momentum)
    components.append(enthalpy_factor * pressure * normal_speed + 0.5 * mass_flux * kinetic)
    return jnp.stack(components, axis=2)

def face_list(node_grid):
    return [node_grid[:, :, :, 0], node_grid[:, :, :, -1], node_grid[:, :, :, :, 0], node_grid[:, :, :, :, -1], node_grid[:, :, :, :, :, 0], node_grid[:, :, :, :, :, -1]]

def lift(faces):
    shape = faces[0].shape[:3] + (NODE1, NODE1, NODE1)
    node_grid = jnp.zeros(shape, jnp.float32)
    node_grid = node_grid.at[:, :, :, 0].add(faces[0]).at[:, :, :, -1].add(faces[1])
    node_grid = node_grid.at[:, :, :, :, 0].add(faces[2]).at[:, :, :, :, -1].add(faces[3])
    node_grid = node_grid.at[:, :, :, :, :, 0].add(faces[4]).at[:, :, :, :, :, -1].add(faces[5])
    return node_grid

def traces(states):
    node_grid = states.reshape(states.shape[0], states.shape[1], 5, NODE1, NODE1, NODE1)
    return jnp.stack([face.reshape(states.shape[0], states.shape[1], -1) for face in face_list(node_grid)], axis=2)

def split_faces(neighbour_faces):
    return [neighbour_faces[:, :, face_index].reshape(neighbour_faces.shape[0], neighbour_faces.shape[1], 5, NODE1, NODE1) for face_index in range(6)]

def tendency(states, neighbour_faces, double_deriv, inv_weight):
    highest = lax.Precision.HIGHEST
    node_grid = states.reshape(states.shape[0], states.shape[1], 5, NODE1, NODE1, NODE1)
    flux_x = flux(node_grid[:, :, :, :, None, :, :], node_grid[:, :, :, None, :, :, :], 0)
    combined = jnp.einsum('il,seailjk->seaijk', double_deriv, flux_x, precision=highest)
    flux_y = flux(node_grid[:, :, :, :, :, None, :], node_grid[:, :, :, :, None, :, :], 1)
    combined = combined + jnp.einsum('jm,seaijmk->seaijk', double_deriv, flux_y, precision=highest)
    flux_z = flux(node_grid[:, :, :, :, :, :, None], node_grid[:, :, :, :, :, None, :], 2)
    combined = combined + jnp.einsum('kn,seaijkn->seaijk', double_deriv, flux_z, precision=highest)
    own_faces = face_list(node_grid)
    other_faces = split_faces(neighbour_faces)
    corrections = []
    for face_index in range(6):
        direction = face_index // 2
        normal_sign = 2.0 * (face_index % 2) - 1.0
        own_face = own_faces[face_index]
        other_face = other_faces[face_index]
        jump = flux(own_face, other_face, direction) - flux(own_face, own_face, direction)
        corrections.append(normal_sign * jump - 0.5 * dissipation * (other_face - own_face))
    combined = combined + inv_weight * lift(corrections)
    return (-2.0 * combined).reshape(states.shape)

def apply_inverse(inverses, vectors):
    return jnp.einsum('epq,seq->sep', inverses, vectors, precision=lax.Precision.HIGHEST)

def reference(u_start, inverses, neighbours, partners):
    double_deriv, inv_weight = lobatto()
    butcher = jnp.asarray(radau_table(), jnp.float32)
    coupling = time_step * jnp.diagonal(butcher) * dissipation * inv_weight
    opposite = [1, 0, 3, 2, 5]

    def gather_faces(face_traces):
        picked = [face_traces[:, neighbours[:, face_index], opposite[face_index]] for face_index in range(5)]
        picked.append(face_traces[:, partners, 4])
        return jnp.stack(picked, axis=2)
    states = jnp.broadcast_to(u_start[None], (SECTIONS,) + u_start.shape).astype(jnp.float32)
    for newton_round in range(NEWTON):
        tendencies = tendency(states, gather_faces(traces(states)), double_deriv, inv_weight)
        coupled = jnp.einsum('ij,jep->iep', butcher, tendencies, precision=lax.Precision.HIGHEST)
        residual = states - u_start[None] - time_step * coupled
        first_sweep = apply_inverse(inverses, -residual)
        lifted = lift(split_faces(gather_faces(traces(first_sweep)))).reshape(states.shape)
        second = apply_inverse(inverses, -residual + coupling[:, None, None] * lifted)
        states = states + second
    return states
```

```python
import functools
import math

import jax
import jax.numpy as jnp
from jax import lax
from jax.experimental import pallas as pl
from jax.experimental.pallas import tpu as pltpu
from jax.sharding import PartitionSpec as P

NODE1 = 4
SECTIONS = 4
NEWTON = 2


time_step = 0.03
dissipation = 2.0
enthalpy_factor = 3.5
radau_nodes = [0.08858795951270394, 0.4094668644407347, 0.787659461760847, 1.0]


def lobatto():
    node_count = NODE1
    inner_value = 1.0 / math.sqrt(5.0)
    lobatto_nodes = [-1.0, -inner_value, inner_value, 1.0]
    products = []
    for row in range(node_count):
        value = 1.0
        for other in range(node_count):
            if other != row:
                value = value * (lobatto_nodes[row] - lobatto_nodes[other])
        products.append(value)
    derivative = []
    for row in range(node_count):
        entries = []
        for column in range(node_count):
            if row == column:
                total = 0.0
                for other in range(node_count):
                    if other != row:
                        total = total + 1.0 / (lobatto_nodes[row] - lobatto_nodes[other])
                entries.append(2.0 * total)
            else:
                entries.append(
                    2.0
                    * (products[row] / products[column])
                    / (lobatto_nodes[row] - lobatto_nodes[column])
                )
        derivative.append(entries)
    return derivative, float(node_count * (node_count - 1) / 2.0)


def radau_table():
    section_total = SECTIONS
    butcher = []
    columns = []
    for column in range(section_total):
        coeffs = [1.0]
        scale = 1.0
        for other in range(section_total):
            if other != column:
                shifted = [0.0] + coeffs
                for position in range(len(coeffs)):
                    shifted[position] = shifted[position] - radau_nodes[other] * coeffs[position]
                coeffs = shifted
                scale = scale * (radau_nodes[column] - radau_nodes[other])
        integral = [0.0] + [
            coeffs[position] / (position + 1.0) / scale for position in range(len(coeffs))
        ]
        columns.append(integral)
    for row in range(section_total):
        entries = []
        for column in range(section_total):
            value = 0.0
            for coefficient in reversed(columns[column]):
                value = value * radau_nodes[row] + coefficient
            entries.append(value)
        butcher.append(entries)
    return butcher


FIELDS = 5
NODES = NODE1**3
FACE = NODE1**2
LANES = 128
SUB = 8
CHUNKS = ((0, 2), (2, 2), (4, 1))
LOADS = ((0, 1), (1, 2), (3, 2))
X_SLOT, Y_SLOT, Z_SLOT = 0, 4, 8
VMEM_BYTES = 54 * 2**20
MESH = pl.DeviceIdType.MESH


def strided(start, count):
    return pl.ds(start, count, stride=NODE1)


def to_k_order(src_ref, k_ref):
    for field in range(FIELDS):
        for k in range(NODE1):
            base = field * NODES
            k_ref[base + k * FACE : base + (k + 1) * FACE, :] = src_ref[strided(base + k, FACE), :]


def slab(src_ref, k_ref, direction, position):
    out = []
    for field in range(FIELDS):
        base = field * NODES
        if direction == 0:
            out.append(src_ref[base + position * FACE : base + (position + 1) * FACE, :])
        elif direction == 1:
            out.append(k_ref[strided(base + position, FACE), :])
        else:
            out.append(k_ref[base + position * FACE : base + (position + 1) * FACE, :])
    return out


def put_slabs(out_ref, k_ref, direction, slabs):
    for position in range(NODE1):
        for field in range(FIELDS):
            base = field * NODES
            rows = slice(base + position * FACE, base + (position + 1) * FACE)
            value = slabs[position][field]
            if direction == 0:
                out_ref[rows, :] = value
            elif direction == 1:
                k_ref[strided(base + position, FACE), :] = value
            else:
                value = k_ref[rows, :] + value
                there = strided(base + position, FACE)
                out_ref[there, :] = out_ref[there, :] + value


def speed2(state):
    return state[1] * state[1] + state[2] * state[2] + state[3] * state[3]


def two_point(a, ka, b, kb, direction):
    r = a[0] + b[0]
    v = [a[1 + c] + b[1 + c] for c in range(3)]
    p = a[4] + b[4]
    n = v[direction]
    m = (0.25 * r) * n
    half = 0.5 * m
    out = [m]
    for c in range(3):
        term = half * v[c]
        if c == direction:
            term = term + 0.5 * p
        out.append(term)
    out.append((0.25 * enthalpy_factor * p) * n + (0.5 * half) * (ka + kb))
    return out


def volume(uc, uk, out_ref, tk, scale):
    deriv, _ = lobatto()
    for direction in range(3):
        states = [slab(uc, uk, direction, pos) for pos in range(NODE1)]
        speeds = [speed2(state) for state in states]
        sums = [None] * NODE1
        for a in range(NODE1):
            for b in range(a + 1, NODE1):
                f = two_point(states[a], speeds[a], states[b], speeds[b], direction)
                for at, other in ((a, b), (b, a)):
                    c = -2.0 * scale * deriv[at][other]
                    terms = [c * x for x in f]
                    sums[at] = terms if sums[at] is None else [x + y for x, y in zip(sums[at], terms)]
        put_slabs(out_ref, tk, direction, sums)


def face_terms(own, other, direction, flux_scale, jump_scale):
    f = two_point(own, speed2(own), other, speed2(other), direction)
    return [flux_scale * x - jump_scale * (n - u) for x, n, u in zip(f, other, own)]


def surface(g, near_ref, out_ref, scale):
    _, inv_weight = lobatto()
    c = -2.0 * scale * inv_weight
    d = 0.5 * dissipation * c
    row = lax.broadcasted_iota(jnp.int32, (SUB, LANES), 0)
    top = row < NODE1
    k = row % NODE1
    y_scale = jnp.where(top, -c, c)
    z_scale = jnp.where(k == 0, -c, jnp.where(k == NODE1 - 1, c, 0.0))
    z_jump = jnp.where((k == 0) | (k == NODE1 - 1), d, 0.0)

    for i in range(NODE1):
        rows = [[g_rows(f, i, half) for f in range(FIELDS)] for half in range(2)]
        own = [[g[rows[half][f], :] for f in range(FIELDS)] for half in range(2)]
        total = [
            face_terms(own[half], near_state(near_ref, Z_SLOT + 2 * i + half), 2, z_scale, z_jump)
            for half in range(2)
        ]
        y_own = [jnp.where(top, low, high) for low, high in zip(*own)]
        y_terms = face_terms(y_own, near_state(near_ref, Y_SLOT + i), 1, y_scale, d)
        total = [
            [t + jnp.where(top if half == 0 else ~top, y, 0.0) for t, y in zip(total[half], y_terms)]
            for half in range(2)
        ]
        if i in (0, NODE1 - 1):
            side = 0 if i == 0 else 1
            for half in range(2):
                x_terms = face_terms(
                    own[half], near_state(near_ref, X_SLOT + 2 * side + half), 0, (2 * side - 1) * c, d
                )
                total[half] = [t + x for t, x in zip(total[half], x_terms)]
        for half in range(2):
            for f in range(FIELDS):
                out_ref[rows[half][f], :] = out_ref[rows[half][f], :] + total[half][f]


def g_rows(f, i, half):
    start = f * NODES + i * FACE + half * SUB
    return slice(start, start + SUB)


def c_rows(f, half):
    start = f * FACE + half * SUB
    return slice(start, start + SUB)


def near_state(near_ref, slot):
    return [near_ref[slot, f] for f in range(FIELDS)]


def take(value, index):
    return jnp.take_along_axis(value, index, axis=1, mode="promise_in_bounds")


def kernel(
    devices, count, u_in, nbr_in, partner_in, inv_ref, out_ref,
    u_ref, nbr_ref, partner_ref,
    raw_ref, tt_ref, y_ref, zsend_ref, recv_ref, zrecv_ref, index_ref, near_v, near_ref,
    uc, uk, vc, wc, lc, tk, gc, x_ref, acc_ref, last_ref,
    in_sem, a_sem, send_sem, recv_sem,
):
    rank = lax.axis_index("elem")
    part = lax.axis_index("section")
    parts = lax.axis_size("section")
    own_sections = SECTIONS // parts
    rotation = devices // 4
    unknowns = FIELDS * NODES
    butcher = radau_table()
    _, inv_weight = lobatto()

    def at(offset):
        return lax.rem(rank + (offset + devices), devices)

    barrier = pltpu.get_barrier_semaphore()
    others = (1, -1, rotation, -rotation, rotation + 1, -rotation - 1)
    for offset in others:
        pl.semaphore_signal(barrier, inc=1, device_id={"elem": at(offset)}, device_id_type=MESH)
    small = [
        pltpu.make_async_copy(src, dst, in_sem.at[index])
        for index, (src, dst) in enumerate(
            ((u_in, u_ref), (nbr_in, nbr_ref), (partner_in, partner_ref))
        )
    ]
    for each in small:
        each.start()

    def load(part_of):
        first, fields = LOADS[part_of]
        rows = pl.ds(first * NODES, fields * NODES)
        for e in range(count):
            pltpu.make_async_copy(inv_ref.at[e, rows], raw_ref.at[rows, e], a_sem.at[part_of]).start()

    def loaded(part_of):
        first, fields = LOADS[part_of]
        there = raw_ref.at[pl.ds(first * NODES, fields * NODES)]
        pltpu.make_async_copy(there, there, a_sem.at[part_of]).wait()

    def transposed(f, r):
        for q in range(0, unknowns, LANES):
            width = min(LANES, unknowns - q)
            blocks = [raw_ref[f * NODES + b * FACE + r, :, q : q + width] for b in range(NODE1)]
            tt_ref[f * FACE + r, q : q + width, :] = jnp.concatenate(blocks, axis=0).T

    load(0)

    row = lax.broadcasted_iota(jnp.int32, (SUB, LANES), 0)
    lane = lax.broadcasted_iota(jnp.int32, (SUB, LANES), 1)
    group = lane // count
    local = lane - group * count
    top = row < NODE1
    k_of = row % NODE1
    block = group[:1]

    def copies(x, chunk):
        first, fields = CHUNKS[chunk]
        rows = pl.ds(first * FACE, fields * FACE)
        zrows = pl.ds(chunk * SUB, SUB)
        out = []
        for which in range(4):
            if which < 2:
                src, dst = y_ref.at[x, rows], recv_ref.at[x, which, rows]
                target = at(1) if which == 0 else at(-1)
            else:
                src, dst = zsend_ref.at[x, zrows], zrecv_ref.at[x, which - 2, zrows]
                target = at(-rotation) if which == 2 else at(-rotation - 1)
            slot = chunk * 4 + which
            out.append(pltpu.make_async_remote_copy(
                src_ref=src, dst_ref=dst, send_sem=send_sem.at[x, slot],
                recv_sem=recv_sem.at[x, slot], device_id={"elem": target}, device_id_type=MESH,
            ))
        return out

    def pack(x, chunk):
        first, fields = CHUNKS[chunk]
        packed = jnp.zeros((SUB, LANES), jnp.float32)
        for slot in range(2 * fields):
            value = y_ref[x, c_rows(first + slot // 2, slot % 2), :]
            value = value if slot == 0 else pltpu.roll(value, slot, 0)
            packed = jnp.where(k_of == slot, value, packed)
        zsend_ref[x, chunk * SUB : (chunk + 1) * SUB, :] = packed

    def send(x, chunk):
        pack(x, chunk)
        out = copies(x, chunk)
        for which in (3, 2, 0, 1):
            out[which].start()

    for each in small:
        each.wait()
    uc[...] = jnp.concatenate([u_ref[...]] * SECTIONS, axis=0).T
    for f in range(FIELDS):
        for half in range(2):
            value = uc[g_rows(f, NODE1 - 1, half), :]
            for i in range(NODE1 - 2, -1, -1):
                value = jnp.where(group == i, uc[g_rows(f, i, half), :], value)
            y_ref[0, c_rows(f, half), :] = value

    load(1)
    load(2)

    def found(wanted, offsets):
        index = wanted - at(offsets[0]) * count
        code = jnp.zeros_like(wanted)
        for at_code, offset in enumerate(offsets[1:]):
            here = wanted - at(offset) * count
            match = (here >= 0) & (here < count)
            index = jnp.where(match, here, index)
            code = jnp.where(match, at_code + 1, code)
        return index, code

    def beside(face):
        wanted = jnp.concatenate([nbr_ref[face : face + 1, :]] * SECTIONS, axis=1)
        return found(jnp.broadcast_to(wanted, (SUB, LANES)), (0, -1, 1))

    per_row = LANES // count
    listed = partner_ref[pl.ds(rank // per_row, 1), :]
    partner = jnp.zeros((1, LANES), jnp.int32)
    for index in range(per_row):
        part_row = jnp.concatenate([listed[:, index * count : (index + 1) * count]] * SECTIONS, axis=1)
        partner = jnp.where(rank % per_row == index, part_row, partner)
    faces = [beside(face) for face in range(5)]
    picks = [
        [
            jnp.where(group == 0, faces[0][0] + (NODE1 - 1) * count, faces[1][0]),
            jnp.where(group == 0, faces[0][1], faces[1][1]),
        ],
        [jnp.where(top, low, high) + shift for low, high, shift in zip(
            faces[2], faces[3], (group * count, 0))],
        [faces[4][0] + group * count, faces[4][1]],
    ]
    index, code = found(jnp.broadcast_to(partner, (SUB, LANES)), (rotation, rotation + 1))
    picks.append([index + group * count, code])
    for kind in range(4):
        for which in range(2):
            index_ref[kind, which] = picks[kind][which]
    spread = [local + i * count for i in range(NODE1)]

    loaded(0)

    @pl.loop(0, FACE)
    def _(r):
        transposed(0, r)

    pl.semaphore_wait(barrier, len(others))
    for chunk in range(len(CHUNKS)):
        send(0, chunk)

    to_k_order(uc, uk)
    volume(uc, uk, lc, tk, 1.0)

    loaded(1)

    @pl.loop(0, FACE)
    def _(r):
        transposed(1, r)
        transposed(2, r)

    loaded(2)

    @pl.loop(0, FACE)
    def _(r):
        transposed(3, r)

    def picked(kind, values):
        index = index_ref[kind, 0]
        code = index_ref[kind, 1]
        out = take(values[0], index)
        for at_code, value in enumerate(values[1:]):
            out = jnp.where(code == at_code + 1, take(value, index), out)
        return out

    def arrived(x, chunk):
        for each in copies(x, chunk):
            each.wait_recv()

    def near_compact(x, chunk):
        first, fields = CHUNKS[chunk]
        out = []
        for each in range(fields):
            f = first + each
            low, high = [
                [y_ref[x, c_rows(f, half), :]]
                + [recv_ref[x, which, c_rows(f, half), :] for which in range(2)]
                for half in range(2)
            ]
            xs = [picked(0, low), picked(0, high)]
            y = picked(1, [pltpu.roll(jnp.where(top, a, b), NODE1, 0) for a, b in zip(low, high)])
            zs = []
            for half, values in enumerate((low, high)):
                minus = picked(2, [pltpu.roll(value, SUB - (NODE1 - 1), 0) for value in values])
                shift = NODE1 - 1 - (2 * each + half)
                packed = [zrecv_ref[x, which, chunk * SUB : (chunk + 1) * SUB, :] for which in range(2)]
                if shift:
                    packed = [pltpu.roll(value, shift, 0) for value in packed]
                plus = picked(3, packed)
                zs.append(jnp.where(k_of == 0, minus, jnp.where(k_of == NODE1 - 1, plus, 0.0)))
            out.append((f, xs, y, zs))
        return out

    def spread_near(near, put):
        for f, xs, y, zs in near:
            for side, i in enumerate((0, NODE1 - 1)):
                for half in range(2):
                    put(X_SLOT + 2 * side + half, f, take(xs[half], spread[i]))
            for i in range(NODE1):
                put(Y_SLOT + i, f, take(y, spread[i]))
                for half in range(2):
                    put(Z_SLOT + 2 * i + half, f, take(zs[half], spread[i]))

    x_side = (group == 0) | (group == NODE1 - 1)

    def lift(near, v, scale=None):
        for f, xs, y, zs in near:
            for half in range(2):
                value = jnp.where(x_side, xs[half], 0.0) + zs[half]
                value = value + jnp.where(top if half == 0 else ~top, y, 0.0)
                if scale is not None:
                    value = scale * value
                for i in range(NODE1):
                    x_ref[v, g_rows(f, i, half), :] = take(value, spread[i])

    def folded(accs):
        for bit in (1, 2, 4):
            low = (row & bit) == 0
            accs = [
                jnp.where(low, a, pltpu.roll(b, bit, 0)) + jnp.where(low, pltpu.roll(a, SUB - bit, 0), b)
                for a, b in zip(accs[::2], accs[1::2])
            ]
        return accs[0]

    def product(t, xs, dst, fields, first, last):
        vectors = len(xs)
        accs = [[None] * SUB for _ in range(vectors)]
        if not first:
            accs = [[acc_ref[v, t, a] for a in range(SUB)] for v in range(vectors)]
        for q in range(fields[0] * SUB, (fields[0] + fields[1]) * SUB):
            rows = slice(q * SUB, (q + 1) * SUB)
            parts_of = [x[rows, :] for x in xs]
            for a in range(SUB):
                m = tt_ref[t * SUB + a, rows, :]
                for v in range(vectors):
                    term = m * parts_of[v]
                    accs[v][a] = term if accs[v][a] is None else accs[v][a] + term
        for v in range(vectors):
            if last:
                dst[v][pl.ds(pl.multiple_of(t * SUB, SUB), SUB), :] = folded(accs[v])
            else:
                for a in range(SUB):
                    acc_ref[v, t, a] = accs[v][a]

    blocks = FIELDS * FACE // SUB

    def whole(xs, dst, sends, beside_of=None):
        for chunk, (first, fields) in enumerate(CHUNKS):
            @pl.loop(2 * first, 2 * (first + fields))
            def _(t):
                product(t, xs, dst, (0, FIELDS), True, True)
                if beside_of is not None and first + fields < FIELDS:
                    beside_of(t)
            for x in sends:
                send(x, chunk)

    def by_chunk(xs, dst, sends, ready):
        for chunk, fields in enumerate(CHUNKS[:-1]):
            ready(chunk)

            @pl.loop(0, blocks)
            def _(t):
                product(t, xs, dst, fields, chunk == 0, False)
        ready(len(CHUNKS) - 1)
        for chunk, (first, fields) in enumerate(CHUNKS):
            @pl.loop(2 * first, 2 * (first + fields))
            def _(t):
                product(t, xs, dst, CHUNKS[-1], False, True)
            for x in sends:
                send(x, chunk)

    def put_first(slot, f, value):
        near_ref[slot, f] = value

    for chunk in range(len(CHUNKS)):
        arrived(0, chunk)
        spread_near(near_compact(0, chunk), put_first)
    surface(uc, near_ref, lc, 1.0)

    def rest(t):
        transposed(FIELDS - 1, 2 * t)
        transposed(FIELDS - 1, 2 * t + 1)

    whole([lc], [y_ref.at[1]], [1], rest)

    def ready_v(chunk):
        arrived(1, chunk)
        near = near_compact(1, chunk)
        lift(near, 0)
        for f, xs, y, zs in near:
            for at_slot, value in enumerate((*xs, y, *zs)):
                near_v[f, at_slot] = value

    by_chunk([x_ref.at[0]], [y_ref.at[2]], [2], ready_v)

    def alpha(i):
        return time_step * sum(butcher[i])

    def coupling(i):
        return time_step * butcher[i][i] * dissipation * inv_weight

    def own(p, s):
        return p * own_sections + s % own_sections

    def per_part(value_of):
        value = jnp.float32(value_of(0))
        for other in range(1, parts):
            value = jnp.where(part == other, jnp.float32(value_of(other)), value)
        return value

    def per_lane(value_of):
        out = jnp.zeros((1, LANES), jnp.float32)
        for s in range(SECTIONS):
            out = jnp.where(block == s, per_part(lambda p, s=s: value_of(p, s)), out)
        return out

    alphas = per_lane(lambda p, s: alpha(s))
    betas = per_lane(lambda p, s: alpha(s) * coupling(s))

    for f in range(FIELDS):
        for half in range(2):
            v, w = y_ref[1, c_rows(f, half), :], y_ref[2, c_rows(f, half), :]
            for i in range(NODE1):
                rows = g_rows(f, i, half)
                vc[rows, :] = take(v, spread[i])
                wc[rows, :] = take(w, spread[i])
    gc[...] = uc[...] + alphas * vc[...] + betas * wc[...]
    to_k_order(gc, uk)
    volume(gc, uk, lc, tk, time_step)

    def add_v(slot, f, value):
        near_ref[slot, f] = near_ref[slot, f] + alphas * value

    def add_w(slot, f, value):
        near_ref[slot, f] = near_ref[slot, f] + betas * value

    for f in range(FIELDS):
        v = [near_v[f, at_slot] for at_slot in range(5)]
        spread_near([(f, v[:2], v[2], v[3:])], add_v)
    for chunk in range(len(CHUNKS)):
        arrived(2, chunk)
        spread_near(near_compact(2, chunk), add_w)
    surface(gc, near_ref, lc, time_step)

    sections = range(own_sections)
    own_alphas = [per_part(lambda p, s=s: alpha(own(p, s))) for s in sections]
    own_betas = [per_part(lambda p, s=s: alpha(own(p, s)) * coupling(own(p, s))) for s in sections]
    own_couplings = [per_part(lambda p, s=s: coupling(own(p, s))) for s in sections]
    weights = [
        [per_lane(lambda p, g, s=s, r=r: butcher[own(p, s)][(g - r) % SECTIONS]) for r in range(SECTIONS)]
        for s in sections
    ]
    tends = [lc[...]]
    for r in range(1, SECTIONS):
        tends.append(pltpu.roll(tends[0], r * count, 1))
    for s in sections:
        total = -(own_alphas[s] * vc[...] + own_betas[s] * wc[...])
        for r in range(SECTIONS):
            total = total + weights[s][r] * tends[r]
        x_ref[s] = total

    operands = [x_ref.at[s] for s in sections]
    whole(operands, [y_ref.at[3 + s] for s in sections], [3 + s for s in sections])

    def ready_first(chunk):
        for s in sections:
            arrived(3 + s, chunk)
            lift(near_compact(3 + s, chunk), s, own_couplings[s])

    by_chunk(operands, [last_ref.at[s] for s in sections], [], ready_first)

    for f in range(FIELDS):
        for half in range(2):
            rows = c_rows(f, half)
            values = [
                own_alphas[s] * y_ref[1, rows, :] + own_betas[s] * y_ref[2, rows, :]
                + y_ref[3 + s, rows, :] + last_ref[s, rows, :]
                for s in sections
            ]
            for i in range(NODE1):
                value = take(values[0], spread[i])
                for s in sections[1:]:
                    value = jnp.where(group == s, take(values[s], spread[i]), value)
                gc[g_rows(f, i, half), :] = value
    rows = gc[...].T
    for s in sections:
        out_ref[s] = rows[s * count : (s + 1) * count]
    for x in range(3 + own_sections):
        for chunk in range(len(CHUNKS)):
            for each in copies(x, chunk):
                each.wait_send()


def on_device(u_start, inverses, neighbours, partners):
    count, unknowns = u_start.shape
    devices = lax.axis_size("elem")
    own_sections = SECTIONS // lax.axis_size("section")
    listed = partners.reshape(-1, LANES)
    exchanges = 3 + own_sections
    column = pltpu.VMEM((unknowns, LANES), jnp.float32)
    compact = FIELDS * FACE
    packed = len(CHUNKS) * SUB
    vmem = pl.BlockSpec(memory_space=pltpu.VMEM)
    change = pl.pallas_call(
        functools.partial(kernel, devices, count),
        out_shape=jax.ShapeDtypeStruct((own_sections, count, unknowns), jnp.float32),
        in_specs=[pl.BlockSpec(memory_space=pl.ANY)] * 4,
        out_specs=vmem,
        scratch_shapes=[
            pltpu.VMEM(u_start.shape, jnp.float32),
            pltpu.VMEM(neighbours.shape[::-1], jnp.int32),
            pltpu.VMEM(listed.shape, jnp.int32),
            pltpu.VMEM((unknowns, count, unknowns), jnp.float32),
            pltpu.VMEM((compact, unknowns, LANES), jnp.float32),
            pltpu.VMEM((exchanges, compact, LANES), jnp.float32),
            pltpu.VMEM((exchanges, packed, LANES), jnp.float32),
            pltpu.VMEM((exchanges, 2, compact, LANES), jnp.float32),
            pltpu.VMEM((exchanges, 2, packed, LANES), jnp.float32),
            pltpu.VMEM((4, 2, SUB, LANES), jnp.int32),
            pltpu.VMEM((FIELDS, 5, SUB, LANES), jnp.float32),
            pltpu.VMEM((16, FIELDS, SUB, LANES), jnp.float32),
        ]
        + [column] * 7
        + [
            pltpu.VMEM((own_sections, unknowns, LANES), jnp.float32),
            pltpu.VMEM((own_sections, compact // SUB, SUB, SUB, LANES), jnp.float32),
            pltpu.VMEM((own_sections, compact, LANES), jnp.float32),
            pltpu.SemaphoreType.DMA((3,)),
            pltpu.SemaphoreType.DMA((len(LOADS),)),
            pltpu.SemaphoreType.DMA((exchanges, 4 * len(CHUNKS))),
            pltpu.SemaphoreType.DMA((exchanges, 4 * len(CHUNKS))),
        ],
        compiler_params=pltpu.CompilerParams(
            collective_id=0, has_side_effects=True, vmem_limit_bytes=VMEM_BYTES
        ),
    )(u_start, neighbours.T, listed, inverses)
    return u_start[None] + change


def solution(mesh):
    placed = (P("elem", None), P("elem", None, None), P("elem", None), P())
    return jax.shard_map(
        on_device, mesh=mesh, in_specs=placed, out_specs=P("section", "elem", None), check_vma=False
    )
```

```python
import functools
import math

import jax
import jax.numpy as jnp
from jax import lax
from jax.experimental import pallas as pl
from jax.experimental.pallas import tpu as pltpu
from jax.sharding import PartitionSpec as P

NODE1 = 4
SECTIONS = 4
NEWTON = 2


time_step = 0.03
dissipation = 2.0
enthalpy_factor = 3.5
radau_nodes = [0.08858795951270394, 0.4094668644407347, 0.787659461760847, 1.0]


def lobatto():
    node_count = NODE1
    inner_value = 1.0 / math.sqrt(5.0)
    lobatto_nodes = [-1.0, -inner_value, inner_value, 1.0]
    products = []
    for row in range(node_count):
        value = 1.0
        for other in range(node_count):
            if other != row:
                value = value * (lobatto_nodes[row] - lobatto_nodes[other])
        products.append(value)
    derivative = []
    for row in range(node_count):
        entries = []
        for column in range(node_count):
            if row == column:
                total = 0.0
                for other in range(node_count):
                    if other != row:
                        total = total + 1.0 / (lobatto_nodes[row] - lobatto_nodes[other])
                entries.append(2.0 * total)
            else:
                entries.append(
                    2.0
                    * (products[row] / products[column])
                    / (lobatto_nodes[row] - lobatto_nodes[column])
                )
        derivative.append(entries)
    return derivative, float(node_count * (node_count - 1) / 2.0)


def radau_table():
    section_total = SECTIONS
    butcher = []
    columns = []
    for column in range(section_total):
        coeffs = [1.0]
        scale = 1.0
        for other in range(section_total):
            if other != column:
                shifted = [0.0] + coeffs
                for position in range(len(coeffs)):
                    shifted[position] = shifted[position] - radau_nodes[other] * coeffs[position]
                coeffs = shifted
                scale = scale * (radau_nodes[column] - radau_nodes[other])
        integral = [0.0] + [
            coeffs[position] / (position + 1.0) / scale for position in range(len(coeffs))
        ]
        columns.append(integral)
    for row in range(section_total):
        entries = []
        for column in range(section_total):
            value = 0.0
            for coefficient in reversed(columns[column]):
                value = value * radau_nodes[row] + coefficient
            entries.append(value)
        butcher.append(entries)
    return butcher


FIELDS = 5
NODES = NODE1**3
FACE = NODE1**2
LANES = 128
SUB = 8
CHUNKS = ((0, 2), (2, 2), (4, 1))
WHOLE = (0, 0, 0)
SPLIT = (0, 1, 2)
LOADS = ((0, 1), (1, 2), (3, 2))
X_SLOT, Y_SLOT, Z_SLOT = 0, 4, 8
VMEM_BYTES = 54 * 2**20
MESH = pl.DeviceIdType.MESH


def strided(start, count):
    return pl.ds(start, count, stride=NODE1)


def to_k_order(src_ref, k_ref):
    for field in range(FIELDS):
        for k in range(NODE1):
            base = field * NODES
            k_ref[base + k * FACE : base + (k + 1) * FACE, :] = src_ref[strided(base + k, FACE), :]


def slab(src_ref, k_ref, direction, position):
    out = []
    for field in range(FIELDS):
        base = field * NODES
        if direction == 0:
            out.append(src_ref[base + position * FACE : base + (position + 1) * FACE, :])
        elif direction == 1:
            out.append(k_ref[strided(base + position, FACE), :])
        else:
            out.append(k_ref[base + position * FACE : base + (position + 1) * FACE, :])
    return out


def put_slabs(out_ref, k_ref, direction, slabs):
    for position in range(NODE1):
        for field in range(FIELDS):
            base = field * NODES
            rows = slice(base + position * FACE, base + (position + 1) * FACE)
            value = slabs[position][field]
            if direction == 0:
                out_ref[rows, :] = value
            elif direction == 1:
                k_ref[strided(base + position, FACE), :] = value
            else:
                value = k_ref[rows, :] + value
                there = strided(base + position, FACE)
                out_ref[there, :] = out_ref[there, :] + value


def speed2(state):
    return state[1] * state[1] + state[2] * state[2] + state[3] * state[3]


def two_point(a, ka, b, kb, direction):
    r = a[0] + b[0]
    v = [a[1 + c] + b[1 + c] for c in range(3)]
    p = a[4] + b[4]
    n = v[direction]
    m = (0.25 * r) * n
    half = 0.5 * m
    out = [m]
    for c in range(3):
        term = half * v[c]
        if c == direction:
            term = term + 0.5 * p
        out.append(term)
    out.append((0.25 * enthalpy_factor * p) * n + (0.5 * half) * (ka + kb))
    return out


def volume(uc, uk, out_ref, tk, scale):
    deriv, _ = lobatto()
    for direction in range(3):
        states = [slab(uc, uk, direction, pos) for pos in range(NODE1)]
        speeds = [speed2(state) for state in states]
        sums = [None] * NODE1
        for a in range(NODE1):
            for b in range(a + 1, NODE1):
                f = two_point(states[a], speeds[a], states[b], speeds[b], direction)
                for at, other in ((a, b), (b, a)):
                    c = -2.0 * scale * deriv[at][other]
                    terms = [c * x for x in f]
                    sums[at] = terms if sums[at] is None else [x + y for x, y in zip(sums[at], terms)]
        put_slabs(out_ref, tk, direction, sums)


def face_terms(own, other, direction, flux_scale, jump_scale):
    f = two_point(own, speed2(own), other, speed2(other), direction)
    return [flux_scale * x - jump_scale * (n - u) for x, n, u in zip(f, other, own)]


def surface(g, near_ref, out_ref, scale):
    _, inv_weight = lobatto()
    c = -2.0 * scale * inv_weight
    d = 0.5 * dissipation * c
    row = lax.broadcasted_iota(jnp.int32, (SUB, LANES), 0)
    top = row < NODE1
    k = row % NODE1
    y_scale = jnp.where(top, -c, c)
    z_scale = jnp.where(k == 0, -c, jnp.where(k == NODE1 - 1, c, 0.0))
    z_jump = jnp.where((k == 0) | (k == NODE1 - 1), d, 0.0)

    for i in range(NODE1):
        rows = [[g_rows(f, i, half) for f in range(FIELDS)] for half in range(2)]
        own = [[g[rows[half][f], :] for f in range(FIELDS)] for half in range(2)]
        total = [
            face_terms(own[half], near_state(near_ref, Z_SLOT + 2 * i + half), 2, z_scale, z_jump)
            for half in range(2)
        ]
        y_own = [jnp.where(top, low, high) for low, high in zip(*own)]
        y_terms = face_terms(y_own, near_state(near_ref, Y_SLOT + i), 1, y_scale, d)
        total = [
            [t + jnp.where(top if half == 0 else ~top, y, 0.0) for t, y in zip(total[half], y_terms)]
            for half in range(2)
        ]
        if i in (0, NODE1 - 1):
            side = 0 if i == 0 else 1
            for half in range(2):
                x_terms = face_terms(
                    own[half], near_state(near_ref, X_SLOT + 2 * side + half), 0, (2 * side - 1) * c, d
                )
                total[half] = [t + x for t, x in zip(total[half], x_terms)]
        for half in range(2):
            for f in range(FIELDS):
                out_ref[rows[half][f], :] = out_ref[rows[half][f], :] + total[half][f]


def g_rows(f, i, half):
    start = f * NODES + i * FACE + half * SUB
    return slice(start, start + SUB)


def c_rows(f, half):
    start = f * FACE + half * SUB
    return slice(start, start + SUB)


def near_state(near_ref, slot):
    return [near_ref[slot, f] for f in range(FIELDS)]


def take(value, index):
    return jnp.take_along_axis(value, index, axis=1, mode="promise_in_bounds")


def kernel(
    devices, count, u_in, nbr_in, partner_in, inv_ref, out_ref,
    u_ref, nbr_ref, partner_ref,
    raw_ref, tt_ref, y_ref, zsend_ref, recv_ref, zrecv_ref, index_ref, near_v, near_z, near_ref,
    uc, uk, vc, wc, lc, tk, gc, x_ref, acc_ref, last_ref, done_ref,
    in_sem, a_sem, send_sem, recv_sem, out_sem,
):
    rank = lax.axis_index("elem")
    part = lax.axis_index("section")
    parts = lax.axis_size("section")
    own_sections = SECTIONS // parts
    rotation = devices // 4
    unknowns = FIELDS * NODES
    butcher = radau_table()
    _, inv_weight = lobatto()

    def at(offset):
        return lax.rem(rank + (offset + devices), devices)

    barrier = pltpu.get_barrier_semaphore()
    others = (1, -1, rotation, -rotation, rotation + 1, -rotation - 1)
    for offset in others:
        pl.semaphore_signal(barrier, inc=1, device_id={"elem": at(offset)}, device_id_type=MESH)
    small = [
        pltpu.make_async_copy(src, dst, in_sem.at[index])
        for index, (src, dst) in enumerate(
            ((u_in, u_ref), (nbr_in, nbr_ref), (partner_in, partner_ref))
        )
    ]
    for each in small:
        each.start()

    def load(part_of):
        first, fields = LOADS[part_of]
        rows = pl.ds(first * NODES, fields * NODES)
        for e in range(count):
            pltpu.make_async_copy(inv_ref.at[e, rows], raw_ref.at[rows, e], a_sem.at[part_of]).start()

    def loaded(part_of):
        first, fields = LOADS[part_of]
        there = raw_ref.at[pl.ds(first * NODES, fields * NODES)]
        pltpu.make_async_copy(there, there, a_sem.at[part_of]).wait()

    def transposed(f, r):
        for q in range(0, unknowns, LANES):
            width = min(LANES, unknowns - q)
            blocks = [raw_ref[f * NODES + b * FACE + r, :, q : q + width] for b in range(NODE1)]
            tt_ref[f * FACE + r, q : q + width, :] = jnp.concatenate(blocks, axis=0).T

    load(0)

    row = lax.broadcasted_iota(jnp.int32, (SUB, LANES), 0)
    lane = lax.broadcasted_iota(jnp.int32, (SUB, LANES), 1)
    group = lane // count
    local = lane - group * count
    top = row < NODE1
    k_of = row % NODE1
    block = group[:1]

    events = [(0, WHOLE), (1, SPLIT), (4, WHOLE)] + [(5, SPLIT)] * own_sections

    def event(x, chunk):
        base, offsets = events[x]
        return base + offsets[chunk]

    def copies(x, chunk):
        first, fields = CHUNKS[chunk]
        rows = pl.ds(first * FACE, fields * FACE)
        zrows = pl.ds(chunk * SUB, SUB)
        out = []
        for which in range(4):
            if which < 2:
                src, dst = y_ref.at[x, rows], recv_ref.at[x, which, rows]
                target = at(1) if which == 0 else at(-1)
            else:
                src, dst = zsend_ref.at[x, zrows], zrecv_ref.at[x, which - 2, zrows]
                target = at(-rotation) if which == 2 else at(-rotation - 1)
            out.append(pltpu.make_async_remote_copy(
                src_ref=src, dst_ref=dst, send_sem=send_sem.at[which // 2],
                recv_sem=recv_sem.at[event(x, chunk)], device_id={"elem": target}, device_id_type=MESH,
            ))
        return out

    def arrived(xs, chunks):
        rows = sum(2 * CHUNKS[chunk][1] * FACE + 2 * SUB for chunk in chunks) * len(xs)
        there = tt_ref.at[0, pl.ds(0, rows)]
        pltpu.make_async_copy(there, there, recv_sem.at[event(xs[0], chunks[0])]).wait()

    def packed_rows(values, k):
        packed = jnp.zeros((SUB, LANES), jnp.float32)
        for slot, value in enumerate(values):
            shift = (slot - k) % SUB
            value = pltpu.roll(value, shift, 0) if shift else value
            packed = jnp.where(k_of == slot, value, packed)
        return packed

    def chunk_rows(chunk):
        first, fields = CHUNKS[chunk]
        return [c_rows(first + slot // 2, slot % 2) for slot in range(2 * fields)]

    def send(x, chunk):
        packed = packed_rows([y_ref[x, rows, :] for rows in chunk_rows(chunk)], 0)
        zsend_ref[x, chunk * SUB : (chunk + 1) * SUB, :] = packed
        out = copies(x, chunk)
        for which in (3, 2, 0, 1):
            out[which].start()

    for each in small:
        each.wait()
    uc[...] = jnp.concatenate([u_ref[...]] * SECTIONS, axis=0).T
    for f in range(FIELDS):
        for half in range(2):
            value = uc[g_rows(f, NODE1 - 1, half), :]
            for i in range(NODE1 - 2, -1, -1):
                value = jnp.where(group == i, uc[g_rows(f, i, half), :], value)
            y_ref[0, c_rows(f, half), :] = value

    load(1)
    load(2)

    def found(wanted, offsets):
        index = wanted - at(offsets[0]) * count
        code = jnp.zeros_like(wanted)
        for at_code, offset in enumerate(offsets[1:]):
            here = wanted - at(offset) * count
            match = (here >= 0) & (here < count)
            index = jnp.where(match, here, index)
            code = jnp.where(match, at_code + 1, code)
        return index, code

    def beside(face):
        wanted = jnp.concatenate([nbr_ref[face : face + 1, :]] * SECTIONS, axis=1)
        return found(jnp.broadcast_to(wanted, (SUB, LANES)), (0, -1, 1))

    per_row = LANES // count
    listed = partner_ref[pl.ds(rank // per_row, 1), :]
    partner = jnp.zeros((1, LANES), jnp.int32)
    for index in range(per_row):
        part_row = jnp.concatenate([listed[:, index * count : (index + 1) * count]] * SECTIONS, axis=1)
        partner = jnp.where(rank % per_row == index, part_row, partner)
    faces = [beside(face) for face in range(5)]
    picks = [
        [
            jnp.where(group == 0, faces[0][0] + (NODE1 - 1) * count, faces[1][0]),
            jnp.where(group == 0, faces[0][1], faces[1][1]),
        ],
        [jnp.where(top, low, high) + shift for low, high, shift in zip(
            faces[2], faces[3], (group * count, 0))],
        [faces[4][0] + group * count, faces[4][1]],
    ]
    index, code = found(jnp.broadcast_to(partner, (SUB, LANES)), (rotation, rotation + 1))
    picks.append([index + group * count, code])
    for kind in range(4):
        for which in range(2):
            index_ref[kind, which] = picks[kind][which]
    pl.semaphore_wait(barrier, len(others))
    for chunk in range(len(CHUNKS)):
        send(0, chunk)

    for part_of, (first, fields) in enumerate(LOADS):
        loaded(part_of)
        for f in range(first, first + fields):
            for r in range(FACE):
                transposed(f, r)

    to_k_order(uc, uk)
    volume(uc, uk, lc, tk, 1.0)

    def picked(kind, values):
        index = index_ref[kind, 0]
        code = index_ref[kind, 1]
        out = take(values[0], index)
        for at_code, value in enumerate(values[1:]):
            out = jnp.where(code == at_code + 1, take(value, index), out)
        return out

    def near_compact(x, chunk):
        first, fields = CHUNKS[chunk]
        sides = []
        for f in range(first, first + fields):
            low, high = [
                [y_ref[x, c_rows(f, half), :]]
                + [recv_ref[x, which, c_rows(f, half), :] for which in range(2)]
                for half in range(2)
            ]
            y = picked(1, [pltpu.roll(jnp.where(top, a, b), NODE1, 0) for a, b in zip(low, high)])
            sides.append((picked(0, low), picked(0, high), y))
        there = chunk_rows(chunk)
        minus = [packed_rows([y_ref[x, rows, :] for rows in there], NODE1 - 1)]
        for which in range(2):
            minus.append(packed_rows([recv_ref[x, which, rows, :] for rows in there], NODE1 - 1))
        plus = [zrecv_ref[x, which, chunk * SUB : (chunk + 1) * SUB, :] for which in range(2)]
        return sides, picked(2, minus), picked(3, plus)

    def spread(value):
        turned = [value] + [pltpu.roll(value, i * count, 1) for i in range(1, NODE1)]
        out = []
        for i in range(NODE1):
            each = turned[(NODE1 - 1 - i) % NODE1]
            for c in range(NODE1 - 2, -1, -1):
                each = jnp.where(group == c, turned[(c - i) % NODE1], each)
            out.append(each)
        return out

    def z_state(minus, plus, slot):
        if slot:
            minus = pltpu.roll(minus, SUB - slot, 0)
        if slot != NODE1 - 1:
            plus = pltpu.roll(plus, NODE1 - 1 - slot, 0)
        return jnp.where(k_of == 0, minus, jnp.where(k_of == NODE1 - 1, plus, 0.0))

    def spread_near(chunk, near, put):
        sides, minus, plus = near
        minus, plus = spread(minus), spread(plus)
        first, fields = CHUNKS[chunk]
        for each, (x_low, x_high, y) in enumerate(sides):
            f = first + each
            for half, value in enumerate((x_low, x_high)):
                out = spread(value)
                for side, i in enumerate((0, NODE1 - 1)):
                    put(X_SLOT + 2 * side + half, f, out[i])
            out = spread(y)
            for i in range(NODE1):
                put(Y_SLOT + i, f, out[i])
                for half in range(2):
                    put(Z_SLOT + 2 * i + half, f, z_state(minus[i], plus[i], 2 * each + half))

    x_side = (group == 0) | (group == NODE1 - 1)

    def lift(chunk, near, v, scale=None):
        sides, minus, plus = near
        first, fields = CHUNKS[chunk]
        for each, (x_low, x_high, y) in enumerate(sides):
            for half, value in enumerate((x_low, x_high)):
                value = jnp.where(x_side, value, 0.0) + z_state(minus, plus, 2 * each + half)
                value = value + jnp.where(top if half == 0 else ~top, y, 0.0)
                if scale is not None:
                    value = scale * value
                out = spread(value)
                for i in range(NODE1):
                    x_ref[v, g_rows(first + each, i, half), :] = out[i]

    def folded(accs):
        for bit in (1, 2, 4):
            low = (row & bit) == 0
            accs = [
                jnp.where(low, a, pltpu.roll(b, bit, 0)) + jnp.where(low, pltpu.roll(a, SUB - bit, 0), b)
                for a, b in zip(accs[::2], accs[1::2])
            ]
        return accs[0]

    def product(t, xs, dst, fields, first, last):
        vectors = len(xs)
        accs = [[None] * SUB for _ in range(vectors)]
        if not first:
            accs = [[acc_ref[v, t, a] for a in range(SUB)] for v in range(vectors)]
        for q in range(fields[0] * SUB, (fields[0] + fields[1]) * SUB):
            rows = slice(q * SUB, (q + 1) * SUB)
            parts_of = [x[rows, :] for x in xs]
            for a in range(SUB):
                m = tt_ref[t * SUB + a, rows, :]
                for v in range(vectors):
                    term = m * parts_of[v]
                    accs[v][a] = term if accs[v][a] is None else accs[v][a] + term
        for v in range(vectors):
            if last:
                dst[v][pl.ds(pl.multiple_of(t * SUB, SUB), SUB), :] = folded(accs[v])
            else:
                for a in range(SUB):
                    acc_ref[v, t, a] = accs[v][a]

    blocks = FIELDS * FACE // SUB

    def whole(xs, dst, sends):
        for chunk, (first, fields) in enumerate(CHUNKS):
            @pl.loop(2 * first, 2 * (first + fields))
            def _(t):
                product(t, xs, dst, (0, FIELDS), True, True)

            for x in sends:
                send(x, chunk)

    def by_chunk(xs, dst, sends, ready):
        for chunk, fields in enumerate(CHUNKS[:-1]):
            ready(chunk)

            @pl.loop(0, blocks)
            def _(t):
                product(t, xs, dst, fields, chunk == 0, False)
        ready(len(CHUNKS) - 1)
        for chunk, (first, fields) in enumerate(CHUNKS):
            @pl.loop(2 * first, 2 * (first + fields))
            def _(t):
                product(t, xs, dst, CHUNKS[-1], False, True)
            for x in sends:
                send(x, chunk)

    def put_first(slot, f, value):
        near_ref[slot, f] = value

    every = range(len(CHUNKS))
    arrived([0], every)
    for chunk in every:
        spread_near(chunk, near_compact(0, chunk), put_first)
    surface(uc, near_ref, lc, 1.0)
    whole([lc], [y_ref.at[1]], [1])

    def ready_v(chunk):
        arrived([1], [chunk])
        near = near_compact(1, chunk)
        lift(chunk, near, 0)
        sides, minus, plus = near
        for each, side in enumerate(sides):
            for slot, value in enumerate(side):
                near_v[CHUNKS[chunk][0] + each, slot] = value
        near_z[chunk, 0] = minus
        near_z[chunk, 1] = plus

    by_chunk([x_ref.at[0]], [y_ref.at[2]], [2], ready_v)

    def alpha(i):
        return time_step * sum(butcher[i])

    def coupling(i):
        return time_step * butcher[i][i] * dissipation * inv_weight

    def own(p, s):
        return p * own_sections + s % own_sections

    def per_part(value_of):
        value = jnp.float32(value_of(0))
        for other in range(1, parts):
            value = jnp.where(part == other, jnp.float32(value_of(other)), value)
        return value

    def per_lane(value_of):
        out = jnp.zeros((1, LANES), jnp.float32)
        for s in range(SECTIONS):
            out = jnp.where(block == s, per_part(lambda p, s=s: value_of(p, s)), out)
        return out

    alphas = per_lane(lambda p, s: alpha(s))
    betas = per_lane(lambda p, s: alpha(s) * coupling(s))

    for f in range(FIELDS):
        for half in range(2):
            v, w = y_ref[1, c_rows(f, half), :], y_ref[2, c_rows(f, half), :]
            for i, (v, w) in enumerate(zip(spread(v), spread(w))):
                rows = g_rows(f, i, half)
                vc[rows, :] = v
                wc[rows, :] = w
    gc[...] = uc[...] + alphas * vc[...] + betas * wc[...]
    to_k_order(gc, uk)
    volume(gc, uk, lc, tk, time_step)

    def add_v(slot, f, value):
        near_ref[slot, f] = near_ref[slot, f] + alphas * value

    def add_w(slot, f, value):
        near_ref[slot, f] = near_ref[slot, f] + betas * value

    for chunk, (first, fields) in enumerate(CHUNKS):
        sides = [[near_v[f, slot] for slot in range(3)] for f in range(first, first + fields)]
        spread_near(chunk, (sides, near_z[chunk, 0], near_z[chunk, 1]), add_v)
    arrived([2], every)
    for chunk in every:
        spread_near(chunk, near_compact(2, chunk), add_w)
    surface(gc, near_ref, lc, time_step)

    sections = range(own_sections)
    own_alphas = [per_part(lambda p, s=s: alpha(own(p, s))) for s in sections]
    own_betas = [per_part(lambda p, s=s: alpha(own(p, s)) * coupling(own(p, s))) for s in sections]
    own_couplings = [per_part(lambda p, s=s: coupling(own(p, s))) for s in sections]
    weights = [
        [per_lane(lambda p, g, s=s, r=r: butcher[own(p, s)][(g - r) % SECTIONS]) for r in range(SECTIONS)]
        for s in sections
    ]
    tends = [lc[...]]
    for r in range(1, SECTIONS):
        tends.append(pltpu.roll(tends[0], r * count, 1))
    for s in sections:
        total = -(own_alphas[s] * vc[...] + own_betas[s] * wc[...])
        for r in range(SECTIONS):
            total = total + weights[s][r] * tends[r]
        x_ref[s] = total

    operands = [x_ref.at[s] for s in sections]
    whole(operands, [y_ref.at[3 + s] for s in sections], [3 + s for s in sections])

    def ready_first(chunk):
        arrived([3 + s for s in sections], [chunk])
        for s in sections:
            lift(chunk, near_compact(3 + s, chunk), s, own_couplings[s])

    by_chunk(operands, [last_ref.at[s] for s in sections], [], ready_first)

    for f in range(FIELDS):
        for half in range(2):
            rows = c_rows(f, half)
            values = [
                own_alphas[s] * y_ref[1, rows, :] + own_betas[s] * y_ref[2, rows, :]
                + y_ref[3 + s, rows, :] + last_ref[s, rows, :]
                for s in sections
            ]
            values = [spread(value) for value in values]
            for i in range(NODE1):
                value = values[0][i]
                for s in sections[1:]:
                    value = jnp.where(group == s, values[s][i], value)
                gc[g_rows(f, i, half), :] = value
    rows = gc[...].T
    for s in sections:
        done_ref[s] = rows[s * count : (s + 1) * count]
    out = pltpu.make_async_copy(done_ref, out_ref, out_sem)
    out.start()
    for which, there in enumerate((recv_ref, zrecv_ref)):
        pltpu.make_async_copy(there, there, send_sem.at[which]).wait()
    out.wait()


def on_device(u_start, inverses, neighbours, partners):
    count, unknowns = u_start.shape
    devices = lax.axis_size("elem")
    own_sections = SECTIONS // lax.axis_size("section")
    listed = partners.reshape(-1, LANES)
    exchanges = 3 + own_sections
    column = pltpu.VMEM((unknowns, LANES), jnp.float32)
    compact = FIELDS * FACE
    packed = len(CHUNKS) * SUB
    change = pl.pallas_call(
        functools.partial(kernel, devices, count),
        out_shape=jax.ShapeDtypeStruct((own_sections, count, unknowns), jnp.float32),
        in_specs=[pl.BlockSpec(memory_space=pl.ANY)] * 4,
        out_specs=pl.BlockSpec(memory_space=pl.ANY),
        scratch_shapes=[
            pltpu.VMEM(u_start.shape, jnp.float32),
            pltpu.VMEM(neighbours.shape[::-1], jnp.int32),
            pltpu.VMEM(listed.shape, jnp.int32),
            pltpu.VMEM((unknowns, count, unknowns), jnp.float32),
            pltpu.VMEM((compact, unknowns, LANES), jnp.float32),
            pltpu.VMEM((exchanges, compact, LANES), jnp.float32),
            pltpu.VMEM((exchanges, packed, LANES), jnp.float32),
            pltpu.VMEM((exchanges, 2, compact, LANES), jnp.float32),
            pltpu.VMEM((exchanges, 2, packed, LANES), jnp.float32),
            pltpu.VMEM((4, 2, SUB, LANES), jnp.int32),
            pltpu.VMEM((FIELDS, 3, SUB, LANES), jnp.float32),
            pltpu.VMEM((len(CHUNKS), 2, SUB, LANES), jnp.float32),
            pltpu.VMEM((16, FIELDS, SUB, LANES), jnp.float32),
        ]
        + [column] * 7
        + [
            pltpu.VMEM((own_sections, unknowns, LANES), jnp.float32),
            pltpu.VMEM((own_sections, compact // SUB, SUB, SUB, LANES), jnp.float32),
            pltpu.VMEM((own_sections, compact, LANES), jnp.float32),
            pltpu.VMEM((own_sections, count, unknowns), jnp.float32),
            pltpu.SemaphoreType.DMA((3,)),
            pltpu.SemaphoreType.DMA((len(LOADS),)),
            pltpu.SemaphoreType.DMA((2,)),
            pltpu.SemaphoreType.DMA((8,)),
            pltpu.SemaphoreType.DMA,
        ],
        compiler_params=pltpu.CompilerParams(
            collective_id=0, has_side_effects=True, vmem_limit_bytes=VMEM_BYTES
        ),
    )(u_start, neighbours.T, listed, inverses)
    return u_start[None] + change


def solution(mesh):
    placed = (P("elem", None), P("elem", None, None), P("elem", None), P())
    return jax.shard_map(
        on_device, mesh=mesh, in_specs=placed, out_specs=P("section", "elem", None), check_vma=False
    )
```

```python
import functools
import math

import jax
import jax.numpy as jnp
from jax import lax
from jax.experimental import pallas as pl
from jax.experimental.pallas import tpu as pltpu
from jax.sharding import PartitionSpec as P

NODE1 = 4
SECTIONS = 4
NEWTON = 2


time_step = 0.03
dissipation = 2.0
enthalpy_factor = 3.5
radau_nodes = [0.08858795951270394, 0.4094668644407347, 0.787659461760847, 1.0]


def lobatto():
    node_count = NODE1
    inner_value = 1.0 / math.sqrt(5.0)
    lobatto_nodes = [-1.0, -inner_value, inner_value, 1.0]
    products = []
    for row in range(node_count):
        value = 1.0
        for other in range(node_count):
            if other != row:
                value = value * (lobatto_nodes[row] - lobatto_nodes[other])
        products.append(value)
    derivative = []
    for row in range(node_count):
        entries = []
        for column in range(node_count):
            if row == column:
                total = 0.0
                for other in range(node_count):
                    if other != row:
                        total = total + 1.0 / (lobatto_nodes[row] - lobatto_nodes[other])
                entries.append(2.0 * total)
            else:
                entries.append(
                    2.0
                    * (products[row] / products[column])
                    / (lobatto_nodes[row] - lobatto_nodes[column])
                )
        derivative.append(entries)
    return derivative, float(node_count * (node_count - 1) / 2.0)


def radau_table():
    section_total = SECTIONS
    butcher = []
    columns = []
    for column in range(section_total):
        coeffs = [1.0]
        scale = 1.0
        for other in range(section_total):
            if other != column:
                shifted = [0.0] + coeffs
                for position in range(len(coeffs)):
                    shifted[position] = shifted[position] - radau_nodes[other] * coeffs[position]
                coeffs = shifted
                scale = scale * (radau_nodes[column] - radau_nodes[other])
        integral = [0.0] + [
            coeffs[position] / (position + 1.0) / scale for position in range(len(coeffs))
        ]
        columns.append(integral)
    for row in range(section_total):
        entries = []
        for column in range(section_total):
            value = 0.0
            for coefficient in reversed(columns[column]):
                value = value * radau_nodes[row] + coefficient
            entries.append(value)
        butcher.append(entries)
    return butcher


FIELDS = 5
NODES = NODE1**3
FACE = NODE1**2
LANES = 128
SUB = 8
CHUNKS = ((0, 2), (2, 2), (4, 1))
WHOLE = (0, 0, 0)
SPLIT = (0, 1, 2)
LOADS = tuple((f, 1) for f in range(5))
X_SLOT, Y_SLOT, Z_SLOT = 0, 4, 8
VMEM_BYTES = 54 * 2**20
MESH = pl.DeviceIdType.MESH


def strided(start, count):
    return pl.ds(start, count, stride=NODE1)


def to_k_order(src_ref, k_ref):
    for field in range(FIELDS):
        for k in range(NODE1):
            base = field * NODES
            k_ref[base + k * FACE : base + (k + 1) * FACE, :] = src_ref[strided(base + k, FACE), :]


def slab(src_ref, k_ref, direction, position):
    out = []
    for field in range(FIELDS):
        base = field * NODES
        if direction == 0:
            out.append(src_ref[base + position * FACE : base + (position + 1) * FACE, :])
        elif direction == 1:
            out.append(k_ref[strided(base + position, FACE), :])
        else:
            out.append(k_ref[base + position * FACE : base + (position + 1) * FACE, :])
    return out


def put_slabs(out_ref, k_ref, direction, slabs):
    for position in range(NODE1):
        for field in range(FIELDS):
            base = field * NODES
            rows = slice(base + position * FACE, base + (position + 1) * FACE)
            value = slabs[position][field]
            if direction == 0:
                out_ref[rows, :] = value
            elif direction == 1:
                k_ref[strided(base + position, FACE), :] = value
            else:
                value = k_ref[rows, :] + value
                there = strided(base + position, FACE)
                out_ref[there, :] = out_ref[there, :] + value


def speed2(state):
    return state[1] * state[1] + state[2] * state[2] + state[3] * state[3]


def two_point(a, ka, b, kb, direction):
    r = a[0] + b[0]
    v = [a[1 + c] + b[1 + c] for c in range(3)]
    p = a[4] + b[4]
    n = v[direction]
    m = (0.25 * r) * n
    half = 0.5 * m
    out = [m]
    for c in range(3):
        term = half * v[c]
        if c == direction:
            term = term + 0.5 * p
        out.append(term)
    out.append((0.25 * enthalpy_factor * p) * n + (0.5 * half) * (ka + kb))
    return out


def volume(uc, uk, out_ref, tk, scale):
    deriv, _ = lobatto()
    for direction in range(3):
        states = [slab(uc, uk, direction, pos) for pos in range(NODE1)]
        speeds = [speed2(state) for state in states]
        sums = [None] * NODE1
        for a in range(NODE1):
            for b in range(a + 1, NODE1):
                f = two_point(states[a], speeds[a], states[b], speeds[b], direction)
                for at, other in ((a, b), (b, a)):
                    c = -2.0 * scale * deriv[at][other]
                    terms = [c * x for x in f]
                    sums[at] = terms if sums[at] is None else [x + y for x, y in zip(sums[at], terms)]
        put_slabs(out_ref, tk, direction, sums)


def face_terms(own, other, direction, flux_scale, jump_scale):
    f = two_point(own, speed2(own), other, speed2(other), direction)
    return [flux_scale * x - jump_scale * (n - u) for x, n, u in zip(f, other, own)]


def surface(g, near_ref, out_ref, scale):
    _, inv_weight = lobatto()
    c = -2.0 * scale * inv_weight
    d = 0.5 * dissipation * c
    row = lax.broadcasted_iota(jnp.int32, (SUB, LANES), 0)
    top = row < NODE1
    k = row % NODE1
    y_scale = jnp.where(top, -c, c)
    z_scale = jnp.where(k == 0, -c, jnp.where(k == NODE1 - 1, c, 0.0))
    z_jump = jnp.where((k == 0) | (k == NODE1 - 1), d, 0.0)

    for i in range(NODE1):
        rows = [[g_rows(f, i, half) for f in range(FIELDS)] for half in range(2)]
        own = [[g[rows[half][f], :] for f in range(FIELDS)] for half in range(2)]
        total = [
            face_terms(own[half], near_state(near_ref, Z_SLOT + 2 * i + half), 2, z_scale, z_jump)
            for half in range(2)
        ]
        y_own = [jnp.where(top, low, high) for low, high in zip(*own)]
        y_terms = face_terms(y_own, near_state(near_ref, Y_SLOT + i), 1, y_scale, d)
        total = [
            [t + jnp.where(top if half == 0 else ~top, y, 0.0) for t, y in zip(total[half], y_terms)]
            for half in range(2)
        ]
        if i in (0, NODE1 - 1):
            side = 0 if i == 0 else 1
            for half in range(2):
                x_terms = face_terms(
                    own[half], near_state(near_ref, X_SLOT + 2 * side + half), 0, (2 * side - 1) * c, d
                )
                total[half] = [t + x for t, x in zip(total[half], x_terms)]
        for half in range(2):
            for f in range(FIELDS):
                out_ref[rows[half][f], :] = out_ref[rows[half][f], :] + total[half][f]


def g_rows(f, i, half):
    start = f * NODES + i * FACE + half * SUB
    return slice(start, start + SUB)


def c_rows(f, half):
    start = f * FACE + half * SUB
    return slice(start, start + SUB)


def near_state(near_ref, slot):
    return [near_ref[slot, f] for f in range(FIELDS)]


def take(value, index):
    return jnp.take_along_axis(value, index, axis=1, mode="promise_in_bounds")


def kernel(
    devices, count, u_in, nbr_in, partner_in, inv_ref, out_ref,
    u_ref, nbr_ref, partner_ref,
    raw_ref, tt_ref, y_ref, zsend_ref, recv_ref, zrecv_ref, index_ref, near_v, near_z, near_ref,
    uc, uk, vc, wc, lc, tk, gc, x_ref, acc_ref, last_ref,
    in_sem, a_sem, send_sem, recv_sem,
):
    rank = lax.axis_index("elem")
    part = lax.axis_index("section")
    parts = lax.axis_size("section")
    own_sections = SECTIONS // parts
    rotation = devices // 4
    unknowns = FIELDS * NODES
    butcher = radau_table()
    _, inv_weight = lobatto()

    def at(offset):
        return lax.rem(rank + (offset + devices), devices)

    barrier = pltpu.get_barrier_semaphore()
    others = (1, -1, rotation, -rotation, rotation + 1, -rotation - 1)
    for offset in others:
        pl.semaphore_signal(barrier, inc=1, device_id={"elem": at(offset)}, device_id_type=MESH)
    small = [
        pltpu.make_async_copy(src, dst, in_sem.at[index])
        for index, (src, dst) in enumerate(
            ((u_in, u_ref), (nbr_in, nbr_ref), (partner_in, partner_ref))
        )
    ]
    for each in small:
        each.start()

    def load(part_of):
        first, fields = LOADS[part_of]
        rows = pl.ds(first * NODES, fields * NODES)
        for e in range(count):
            pltpu.make_async_copy(inv_ref.at[e, rows], raw_ref.at[rows, e], a_sem.at[part_of]).start()

    def loaded(part_of):
        first, fields = LOADS[part_of]
        there = raw_ref.at[pl.ds(first * NODES, fields * NODES)]
        pltpu.make_async_copy(there, there, a_sem.at[part_of]).wait()

    def transposed(f, r):
        for q in range(0, unknowns, LANES):
            width = min(LANES, unknowns - q)
            blocks = [raw_ref[f * NODES + b * FACE + r, :, q : q + width] for b in range(NODE1)]
            tt_ref[f * FACE + r, q : q + width, :] = jnp.concatenate(blocks, axis=0).T

    load(0)
    load(1)

    row = lax.broadcasted_iota(jnp.int32, (SUB, LANES), 0)
    lane = lax.broadcasted_iota(jnp.int32, (SUB, LANES), 1)
    group = lane // count
    local = lane - group * count
    top = row < NODE1
    k_of = row % NODE1
    block = group[:1]

    events = [(0, WHOLE), (1, SPLIT), (4, WHOLE)] + [(5, SPLIT)] * own_sections

    def event(x, chunk):
        base, offsets = events[x]
        return base + offsets[chunk]

    def copies(x, chunk):
        first, fields = CHUNKS[chunk]
        rows = pl.ds(first * FACE, fields * FACE)
        zrows = pl.ds(chunk * SUB, SUB)
        out = []
        for which in range(4):
            if which < 2:
                src, dst = y_ref.at[x, rows], recv_ref.at[x, which, rows]
                target = at(1) if which == 0 else at(-1)
            else:
                src, dst = zsend_ref.at[x, zrows], zrecv_ref.at[x, which - 2, zrows]
                target = at(-rotation) if which == 2 else at(-rotation - 1)
            out.append(pltpu.make_async_remote_copy(
                src_ref=src, dst_ref=dst, send_sem=send_sem.at[which // 2],
                recv_sem=recv_sem.at[event(x, chunk)], device_id={"elem": target}, device_id_type=MESH,
            ))
        return out

    def arrived(xs, chunks):
        rows = sum(2 * CHUNKS[chunk][1] * FACE + 2 * SUB for chunk in chunks) * len(xs)
        there = tt_ref.at[0, pl.ds(0, rows)]
        pltpu.make_async_copy(there, there, recv_sem.at[event(xs[0], chunks[0])]).wait()

    def packed_rows(values, k):
        packed = jnp.zeros((SUB, LANES), jnp.float32)
        for slot, value in enumerate(values):
            shift = (slot - k) % SUB
            value = pltpu.roll(value, shift, 0) if shift else value
            packed = jnp.where(k_of == slot, value, packed)
        return packed

    def chunk_rows(chunk):
        first, fields = CHUNKS[chunk]
        return [c_rows(first + slot // 2, slot % 2) for slot in range(2 * fields)]

    def send(x, chunk):
        packed = packed_rows([y_ref[x, rows, :] for rows in chunk_rows(chunk)], 0)
        zsend_ref[x, chunk * SUB : (chunk + 1) * SUB, :] = packed
        out = copies(x, chunk)
        for which in (0, 1, 3, 2):
            out[which].start()

    for each in small:
        each.wait()
    uc[...] = jnp.concatenate([u_ref[...]] * SECTIONS, axis=0).T
    for f in range(FIELDS):
        for half in range(2):
            value = uc[g_rows(f, NODE1 - 1, half), :]
            for i in range(NODE1 - 2, -1, -1):
                value = jnp.where(group == i, uc[g_rows(f, i, half), :], value)
            y_ref[0, c_rows(f, half), :] = value

    for part_of in range(2, len(LOADS)):
        load(part_of)

    def found(wanted, offsets):
        index = wanted - at(offsets[0]) * count
        code = jnp.zeros_like(wanted)
        for at_code, offset in enumerate(offsets[1:]):
            here = wanted - at(offset) * count
            match = (here >= 0) & (here < count)
            index = jnp.where(match, here, index)
            code = jnp.where(match, at_code + 1, code)
        return index, code

    def beside(face):
        wanted = jnp.concatenate([nbr_ref[face : face + 1, :]] * SECTIONS, axis=1)
        return found(jnp.broadcast_to(wanted, (SUB, LANES)), (0, -1, 1))

    per_row = LANES // count
    listed = partner_ref[pl.ds(rank // per_row, 1), :]
    partner = jnp.zeros((1, LANES), jnp.int32)
    for index in range(per_row):
        part_row = jnp.concatenate([listed[:, index * count : (index + 1) * count]] * SECTIONS, axis=1)
        partner = jnp.where(rank % per_row == index, part_row, partner)
    faces = [beside(face) for face in range(5)]
    picks = [
        [
            jnp.where(group == 0, faces[0][0] + (NODE1 - 1) * count, faces[1][0]),
            jnp.where(group == 0, faces[0][1], faces[1][1]),
        ],
        [jnp.where(top, low, high) + shift for low, high, shift in zip(
            faces[2], faces[3], (group * count, 0))],
        [faces[4][0] + group * count, faces[4][1]],
    ]
    index, code = found(jnp.broadcast_to(partner, (SUB, LANES)), (rotation, rotation + 1))
    picks.append([index + group * count, code])
    for kind in range(4):
        for which in range(2):
            index_ref[kind, which] = picks[kind][which]
    loaded(0)
    for r in range(FACE // 2):
        transposed(0, r)
    pl.semaphore_wait(barrier, len(others))
    for chunk in range(len(CHUNKS)):
        send(0, chunk)
    for r in range(FACE // 2, FACE):
        transposed(0, r)
    for f in range(1, FIELDS):
        loaded(f)
        for r in range(FACE):
            transposed(f, r)
    to_k_order(uc, uk)
    volume(uc, uk, lc, tk, 1.0)

    def picked(kind, values):
        index = index_ref[kind, 0]
        code = index_ref[kind, 1]
        out = take(values[0], index)
        for at_code, value in enumerate(values[1:]):
            out = jnp.where(code == at_code + 1, take(value, index), out)
        return out

    def near_compact(x, chunk):
        first, fields = CHUNKS[chunk]
        sides = []
        for f in range(first, first + fields):
            low, high = [
                [y_ref[x, c_rows(f, half), :]]
                + [recv_ref[x, which, c_rows(f, half), :] for which in range(2)]
                for half in range(2)
            ]
            y = picked(1, [pltpu.roll(jnp.where(top, a, b), NODE1, 0) for a, b in zip(low, high)])
            sides.append((picked(0, low), picked(0, high), y))
        there = chunk_rows(chunk)
        minus = [packed_rows([y_ref[x, rows, :] for rows in there], NODE1 - 1)]
        for which in range(2):
            minus.append(packed_rows([recv_ref[x, which, rows, :] for rows in there], NODE1 - 1))
        plus = [zrecv_ref[x, which, chunk * SUB : (chunk + 1) * SUB, :] for which in range(2)]
        return sides, picked(2, minus), picked(3, plus)

    def spread(value):
        turned = [value] + [pltpu.roll(value, i * count, 1) for i in range(1, NODE1)]
        out = []
        for i in range(NODE1):
            each = turned[(NODE1 - 1 - i) % NODE1]
            for c in range(NODE1 - 2, -1, -1):
                each = jnp.where(group == c, turned[(c - i) % NODE1], each)
            out.append(each)
        return out

    def z_state(minus, plus, slot):
        if slot:
            minus = pltpu.roll(minus, SUB - slot, 0)
        if slot != NODE1 - 1:
            plus = pltpu.roll(plus, NODE1 - 1 - slot, 0)
        return jnp.where(k_of == 0, minus, jnp.where(k_of == NODE1 - 1, plus, 0.0))

    def spread_near(chunk, near, put):
        sides, minus, plus = near
        minus, plus = spread(minus), spread(plus)
        first, fields = CHUNKS[chunk]
        for each, (x_low, x_high, y) in enumerate(sides):
            f = first + each
            for half, value in enumerate((x_low, x_high)):
                out = spread(value)
                for side, i in enumerate((0, NODE1 - 1)):
                    put(X_SLOT + 2 * side + half, f, out[i])
            out = spread(y)
            for i in range(NODE1):
                put(Y_SLOT + i, f, out[i])
                for half in range(2):
                    put(Z_SLOT + 2 * i + half, f, z_state(minus[i], plus[i], 2 * each + half))

    x_side = (group == 0) | (group == NODE1 - 1)

    def lift(chunk, near, v, scale=None):
        sides, minus, plus = near
        first, fields = CHUNKS[chunk]
        for each, (x_low, x_high, y) in enumerate(sides):
            for half, value in enumerate((x_low, x_high)):
                value = jnp.where(x_side, value, 0.0) + z_state(minus, plus, 2 * each + half)
                value = value + jnp.where(top if half == 0 else ~top, y, 0.0)
                if scale is not None:
                    value = scale * value
                out = spread(value)
                for i in range(NODE1):
                    x_ref[v, g_rows(first + each, i, half), :] = out[i]

    def folded(accs):
        for bit in (1, 2, 4):
            low = (row & bit) == 0
            accs = [
                jnp.where(low, a, pltpu.roll(b, bit, 0)) + jnp.where(low, pltpu.roll(a, SUB - bit, 0), b)
                for a, b in zip(accs[::2], accs[1::2])
            ]
        return accs[0]

    def product(t, xs, dst, fields, first, last):
        vectors = len(xs)
        accs = [[None] * SUB for _ in range(vectors)]
        if not first:
            accs = [[acc_ref[v, t, a] for a in range(SUB)] for v in range(vectors)]
        for q in range(fields[0] * SUB, (fields[0] + fields[1]) * SUB):
            rows = slice(q * SUB, (q + 1) * SUB)
            parts_of = [x[rows, :] for x in xs]
            for a in range(SUB):
                m = tt_ref[t * SUB + a, rows, :]
                for v in range(vectors):
                    term = m * parts_of[v]
                    accs[v][a] = term if accs[v][a] is None else accs[v][a] + term
        for v in range(vectors):
            if last:
                dst[v][pl.ds(pl.multiple_of(t * SUB, SUB), SUB), :] = folded(accs[v])
            else:
                for a in range(SUB):
                    acc_ref[v, t, a] = accs[v][a]

    blocks = FIELDS * FACE // SUB

    def whole(xs, dst, sends):
        for chunk, (first, fields) in enumerate(CHUNKS):
            @pl.loop(2 * first, 2 * (first + fields))
            def _(t):
                product(t, xs, dst, (0, FIELDS), True, True)

            for x in sends:
                send(x, chunk)

    def by_chunk(xs, dst, sends, await_chunk, ready):
        await_chunk(0)
        ready(0)
        for chunk, fields in enumerate(CHUNKS[:-1]):
            await_chunk(chunk + 1)
            ready(chunk + 1)
            for t in range(blocks):
                product(t, xs, dst, fields, chunk == 0, False)
        for chunk, (first, fields) in enumerate(CHUNKS):
            @pl.loop(2 * first, 2 * (first + fields))
            def _(t):
                product(t, xs, dst, CHUNKS[-1], False, True)
            for x in sends:
                send(x, chunk)

    def put_first(slot, f, value):
        near_ref[slot, f] = value

    every = range(len(CHUNKS))
    arrived([0], every)
    for chunk in every:
        spread_near(chunk, near_compact(0, chunk), put_first)
    surface(uc, near_ref, lc, 1.0)
    whole([lc], [y_ref.at[1]], [1])

    def ready_v(chunk):
        near = near_compact(1, chunk)
        lift(chunk, near, 0)
        sides, minus, plus = near
        for each, side in enumerate(sides):
            for slot, value in enumerate(side):
                near_v[CHUNKS[chunk][0] + each, slot] = value
        near_z[chunk, 0] = minus
        near_z[chunk, 1] = plus

    by_chunk([x_ref.at[0]], [y_ref.at[2]], [2], lambda chunk: arrived([1], [chunk]), ready_v)

    def alpha(i):
        return time_step * sum(butcher[i])

    def coupling(i):
        return time_step * butcher[i][i] * dissipation * inv_weight

    def own(p, s):
        return p * own_sections + s % own_sections

    def per_part(value_of):
        value = jnp.float32(value_of(0))
        for other in range(1, parts):
            value = jnp.where(part == other, jnp.float32(value_of(other)), value)
        return value

    def per_lane(value_of):
        out = jnp.zeros((1, LANES), jnp.float32)
        for s in range(SECTIONS):
            out = jnp.where(block == s, per_part(lambda p, s=s: value_of(p, s)), out)
        return out

    alphas = per_lane(lambda p, s: alpha(s))
    betas = per_lane(lambda p, s: alpha(s) * coupling(s))

    for f in range(FIELDS):
        for half in range(2):
            v, w = y_ref[1, c_rows(f, half), :], y_ref[2, c_rows(f, half), :]
            for i, (v, w) in enumerate(zip(spread(v), spread(w))):
                rows = g_rows(f, i, half)
                vc[rows, :] = v
                wc[rows, :] = w
    gc[...] = uc[...] + alphas * vc[...] + betas * wc[...]
    to_k_order(gc, uk)
    volume(gc, uk, lc, tk, time_step)

    def add_v(slot, f, value):
        near_ref[slot, f] = near_ref[slot, f] + alphas * value

    def add_w(slot, f, value):
        near_ref[slot, f] = near_ref[slot, f] + betas * value

    for chunk, (first, fields) in enumerate(CHUNKS):
        sides = [[near_v[f, slot] for slot in range(3)] for f in range(first, first + fields)]
        spread_near(chunk, (sides, near_z[chunk, 0], near_z[chunk, 1]), add_v)
    sections = range(own_sections)
    own_alphas = [per_part(lambda p, s=s: alpha(own(p, s))) for s in sections]
    own_betas = [per_part(lambda p, s=s: alpha(own(p, s)) * coupling(own(p, s))) for s in sections]
    own_couplings = [per_part(lambda p, s=s: coupling(own(p, s))) for s in sections]
    weights = [
        [per_lane(lambda p, g, s=s, r=r: butcher[own(p, s)][(g - r) % SECTIONS]) for r in range(SECTIONS)]
        for s in sections
    ]
    for s in sections:
        x_ref[s] = -(own_alphas[s] * vc[...] + own_betas[s] * wc[...])
    arrived([2], every)
    for chunk in every:
        spread_near(chunk, near_compact(2, chunk), add_w)
    surface(gc, near_ref, lc, time_step)

    for start in range(0, unknowns, SUB):
        rows = slice(start, start + SUB)
        tend = lc[rows, :]
        turned = [tend] + [pltpu.roll(tend, r * count, 1) for r in range(1, SECTIONS)]
        for s in sections:
            total = x_ref[s, rows, :]
            for r in range(SECTIONS):
                total = total + weights[s][r] * turned[r]
            x_ref[s, rows, :] = total

    operands = [x_ref.at[s] for s in sections]
    whole(operands, [y_ref.at[3 + s] for s in sections], [3 + s for s in sections])

    def await_first(chunk):
        arrived([3 + s for s in sections], [chunk])

    def ready_first(chunk):
        for s in sections:
            lift(chunk, near_compact(3 + s, chunk), s, own_couplings[s])

    by_chunk(operands, [last_ref.at[s] for s in sections], [], await_first, ready_first)

    for f in range(FIELDS):
        for half in range(2):
            rows = c_rows(f, half)
            values = [
                own_alphas[s] * y_ref[1, rows, :] + own_betas[s] * y_ref[2, rows, :]
                + y_ref[3 + s, rows, :] + last_ref[s, rows, :]
                for s in sections
            ]
            values = [spread(value) for value in values]
            for i in range(NODE1):
                value = values[0][i]
                for s in sections[1:]:
                    value = jnp.where(group == s, values[s][i], value)
                gc[g_rows(f, i, half), :] = value
    rows = gc[...].T
    for s in sections:
        out_ref[s] = rows[s * count : (s + 1) * count]
    for which, there in enumerate((recv_ref, zrecv_ref)):
        pltpu.make_async_copy(there, there, send_sem.at[which]).wait()


def on_device(u_start, inverses, neighbours, partners):
    count, unknowns = u_start.shape
    devices = lax.axis_size("elem")
    own_sections = SECTIONS // lax.axis_size("section")
    listed = partners.reshape(-1, LANES)
    exchanges = 3 + own_sections
    column = pltpu.VMEM((unknowns, LANES), jnp.float32)
    compact = FIELDS * FACE
    packed = len(CHUNKS) * SUB
    change = pl.pallas_call(
        functools.partial(kernel, devices, count),
        out_shape=pltpu.VMEM((own_sections, count, unknowns), jnp.float32),
        in_specs=[pl.BlockSpec(memory_space=pl.ANY)] * 4,
        out_specs=pl.BlockSpec(memory_space=pltpu.VMEM),
        scratch_shapes=[
            pltpu.VMEM(u_start.shape, jnp.float32),
            pltpu.VMEM(neighbours.shape[::-1], jnp.int32),
            pltpu.VMEM(listed.shape, jnp.int32),
            pltpu.VMEM((unknowns, count, unknowns), jnp.float32),
            pltpu.VMEM((compact, unknowns, LANES), jnp.float32),
            pltpu.VMEM((exchanges, compact, LANES), jnp.float32),
            pltpu.VMEM((exchanges, packed, LANES), jnp.float32),
            pltpu.VMEM((exchanges, 2, compact, LANES), jnp.float32),
            pltpu.VMEM((exchanges, 2, packed, LANES), jnp.float32),
            pltpu.VMEM((4, 2, SUB, LANES), jnp.int32),
            pltpu.VMEM((FIELDS, 3, SUB, LANES), jnp.float32),
            pltpu.VMEM((len(CHUNKS), 2, SUB, LANES), jnp.float32),
            pltpu.VMEM((16, FIELDS, SUB, LANES), jnp.float32),
        ]
        + [column] * 7
        + [
            pltpu.VMEM((own_sections, unknowns, LANES), jnp.float32),
            pltpu.VMEM((own_sections, compact // SUB, SUB, SUB, LANES), jnp.float32),
            pltpu.VMEM((own_sections, compact, LANES), jnp.float32),
            pltpu.SemaphoreType.DMA((3,)),
            pltpu.SemaphoreType.DMA((len(LOADS),)),
            pltpu.SemaphoreType.DMA((2,)),
            pltpu.SemaphoreType.DMA((8,)),
        ],
        compiler_params=pltpu.CompilerParams(
            collective_id=0, has_side_effects=True, vmem_limit_bytes=VMEM_BYTES
        ),
    )(u_start, neighbours.T, listed, inverses)
    return u_start[None] + change


def solution(mesh):
    placed = (P("elem", None), P("elem", None, None), P("elem", None), P())
    return jax.shard_map(
        on_device, mesh=mesh, in_specs=placed, out_specs=P("section", "elem", None), check_vma=False
    )
```

```python
import functools
import math

import jax
import jax.numpy as jnp
from jax import lax
from jax.experimental import pallas as pl
from jax.experimental.pallas import tpu as pltpu
from jax.sharding import PartitionSpec as P

NODE1 = 4
SECTIONS = 4
NEWTON = 2


time_step = 0.03
dissipation = 2.0
enthalpy_factor = 3.5
radau_nodes = [0.08858795951270394, 0.4094668644407347, 0.787659461760847, 1.0]


def lobatto():
    node_count = NODE1
    inner_value = 1.0 / math.sqrt(5.0)
    lobatto_nodes = [-1.0, -inner_value, inner_value, 1.0]
    products = []
    for row in range(node_count):
        value = 1.0
        for other in range(node_count):
            if other != row:
                value = value * (lobatto_nodes[row] - lobatto_nodes[other])
        products.append(value)
    derivative = []
    for row in range(node_count):
        entries = []
        for column in range(node_count):
            if row == column:
                total = 0.0
                for other in range(node_count):
                    if other != row:
                        total = total + 1.0 / (lobatto_nodes[row] - lobatto_nodes[other])
                entries.append(2.0 * total)
            else:
                entries.append(
                    2.0
                    * (products[row] / products[column])
                    / (lobatto_nodes[row] - lobatto_nodes[column])
                )
        derivative.append(entries)
    return derivative, float(node_count * (node_count - 1) / 2.0)


def radau_table():
    section_total = SECTIONS
    butcher = []
    columns = []
    for column in range(section_total):
        coeffs = [1.0]
        scale = 1.0
        for other in range(section_total):
            if other != column:
                shifted = [0.0] + coeffs
                for position in range(len(coeffs)):
                    shifted[position] = shifted[position] - radau_nodes[other] * coeffs[position]
                coeffs = shifted
                scale = scale * (radau_nodes[column] - radau_nodes[other])
        integral = [0.0] + [
            coeffs[position] / (position + 1.0) / scale for position in range(len(coeffs))
        ]
        columns.append(integral)
    for row in range(section_total):
        entries = []
        for column in range(section_total):
            value = 0.0
            for coefficient in reversed(columns[column]):
                value = value * radau_nodes[row] + coefficient
            entries.append(value)
        butcher.append(entries)
    return butcher


FIELDS = 5
NODES = NODE1**3
FACE = NODE1**2
LANES = 128
SUB = 8
CHUNKS = ((0, 2), (2, 2), (4, 1))
FINE = tuple((f, 1) for f in range(5))
SPLIT_AT = 10
LOADS = tuple((f, 1) for f in range(5))
X_SLOT, Y_SLOT, Z_SLOT = 0, 4, 8
VMEM_BYTES = 54 * 2**20
MESH = pl.DeviceIdType.MESH


def strided(start, count):
    return pl.ds(start, count, stride=NODE1)


def to_k_order(src_ref, k_ref):
    for field in range(FIELDS):
        for k in range(NODE1):
            base = field * NODES
            k_ref[base + k * FACE : base + (k + 1) * FACE, :] = src_ref[strided(base + k, FACE), :]


def slab(src_ref, k_ref, direction, position):
    out = []
    for field in range(FIELDS):
        base = field * NODES
        if direction == 0:
            out.append(src_ref[base + position * FACE : base + (position + 1) * FACE, :])
        elif direction == 1:
            out.append(k_ref[strided(base + position, FACE), :])
        else:
            out.append(k_ref[base + position * FACE : base + (position + 1) * FACE, :])
    return out


def put_slabs(out_ref, k_ref, direction, slabs):
    for position in range(NODE1):
        for field in range(FIELDS):
            base = field * NODES
            rows = slice(base + position * FACE, base + (position + 1) * FACE)
            value = slabs[position][field]
            if direction == 0:
                out_ref[rows, :] = value
            elif direction == 1:
                k_ref[strided(base + position, FACE), :] = value
            else:
                value = k_ref[rows, :] + value
                there = strided(base + position, FACE)
                out_ref[there, :] = out_ref[there, :] + value


def speed2(state):
    return state[1] * state[1] + state[2] * state[2] + state[3] * state[3]


def two_point(a, ka, b, kb, direction):
    r = a[0] + b[0]
    v = [a[1 + c] + b[1 + c] for c in range(3)]
    p = a[4] + b[4]
    n = v[direction]
    m = (0.25 * r) * n
    half = 0.5 * m
    out = [m]
    for c in range(3):
        term = half * v[c]
        if c == direction:
            term = term + 0.5 * p
        out.append(term)
    out.append((0.25 * enthalpy_factor * p) * n + (0.5 * half) * (ka + kb))
    return out


def volume(uc, uk, out_ref, tk, scale):
    deriv, _ = lobatto()
    for direction in range(3):
        states = [slab(uc, uk, direction, pos) for pos in range(NODE1)]
        speeds = [speed2(state) for state in states]
        sums = [None] * NODE1
        for a in range(NODE1):
            for b in range(a + 1, NODE1):
                f = two_point(states[a], speeds[a], states[b], speeds[b], direction)
                for at, other in ((a, b), (b, a)):
                    c = -2.0 * scale * deriv[at][other]
                    terms = [c * x for x in f]
                    sums[at] = terms if sums[at] is None else [x + y for x, y in zip(sums[at], terms)]
        put_slabs(out_ref, tk, direction, sums)


def face_terms(own, other, direction, flux_scale, jump_scale):
    f = two_point(own, speed2(own), other, speed2(other), direction)
    return [flux_scale * x - jump_scale * (n - u) for x, n, u in zip(f, other, own)]


def surface(g, near_ref, out_ref, scale):
    _, inv_weight = lobatto()
    c = -2.0 * scale * inv_weight
    d = 0.5 * dissipation * c
    row = lax.broadcasted_iota(jnp.int32, (SUB, LANES), 0)
    top = row < NODE1
    k = row % NODE1
    y_scale = jnp.where(top, -c, c)
    z_scale = jnp.where(k == 0, -c, jnp.where(k == NODE1 - 1, c, 0.0))
    z_jump = jnp.where((k == 0) | (k == NODE1 - 1), d, 0.0)

    for i in range(NODE1):
        rows = [[g_rows(f, i, half) for f in range(FIELDS)] for half in range(2)]
        own = [[g[rows[half][f], :] for f in range(FIELDS)] for half in range(2)]
        total = [
            face_terms(own[half], near_state(near_ref, Z_SLOT + 2 * i + half), 2, z_scale, z_jump)
            for half in range(2)
        ]
        y_own = [jnp.where(top, low, high) for low, high in zip(*own)]
        y_terms = face_terms(y_own, near_state(near_ref, Y_SLOT + i), 1, y_scale, d)
        total = [
            [t + jnp.where(top if half == 0 else ~top, y, 0.0) for t, y in zip(total[half], y_terms)]
            for half in range(2)
        ]
        if i in (0, NODE1 - 1):
            side = 0 if i == 0 else 1
            for half in range(2):
                x_terms = face_terms(
                    own[half], near_state(near_ref, X_SLOT + 2 * side + half), 0, (2 * side - 1) * c, d
                )
                total[half] = [t + x for t, x in zip(total[half], x_terms)]
        for half in range(2):
            for f in range(FIELDS):
                out_ref[rows[half][f], :] = out_ref[rows[half][f], :] + total[half][f]


def g_rows(f, i, half):
    start = f * NODES + i * FACE + half * SUB
    return slice(start, start + SUB)


def c_rows(f, half):
    start = f * FACE + half * SUB
    return slice(start, start + SUB)


def chunks_of(x):
    return FINE if x > 2 else CHUNKS


def near_state(near_ref, slot):
    return [near_ref[slot, f] for f in range(FIELDS)]


def take(value, index):
    return jnp.take_along_axis(value, index, axis=1, mode="promise_in_bounds")


def kernel(
    devices, count, u_in, nbr_in, partner_in, inv_ref, out_ref,
    u_ref, nbr_ref, partner_ref,
    raw_ref, tt_ref, y_ref, zsend_ref, recv_ref, zrecv_ref, index_ref, near_v, near_z, near_ref, own_ref, own_z,
    uc, uk, vc, wc, lc, tk, gc, x_ref, acc_ref, last_ref, eye_ref,
    in_sem, a_sem, send_sem, recv_sem,
):
    rank = lax.axis_index("elem")
    part = lax.axis_index("section")
    parts = lax.axis_size("section")
    own_sections = SECTIONS // parts
    rotation = devices // 4
    unknowns = FIELDS * NODES
    butcher = radau_table()
    _, inv_weight = lobatto()

    def at(offset):
        return lax.rem(rank + (offset + devices), devices)

    barrier = pltpu.get_barrier_semaphore()
    others = (1, -1, rotation, -rotation, rotation + 1, -rotation - 1)
    for offset in others:
        pl.semaphore_signal(barrier, inc=1, device_id={"elem": at(offset)}, device_id_type=MESH)
    small = [
        pltpu.make_async_copy(src, dst, in_sem.at[index])
        for index, (src, dst) in enumerate(
            ((u_in, u_ref), (nbr_in, nbr_ref), (partner_in, partner_ref))
        )
    ]
    for each in small:
        each.start()

    def load(part_of):
        first, fields = LOADS[part_of]
        rows = pl.ds(first * NODES, fields * NODES)
        for e in range(count):
            pltpu.make_async_copy(inv_ref.at[e, rows], raw_ref.at[rows, e], a_sem.at[part_of]).start()

    def loaded(part_of):
        first, fields = LOADS[part_of]
        there = raw_ref.at[pl.ds(first * NODES, fields * NODES)]
        pltpu.make_async_copy(there, there, a_sem.at[part_of]).wait()

    def transposed(f, r):
        for q in range(0, unknowns, LANES):
            width = min(LANES, unknowns - q)
            blocks = [raw_ref[f * NODES + b * FACE + r, :, q : q + width] for b in range(NODE1)]
            tt_ref[f * FACE + r, q : q + width, :] = jnp.concatenate(blocks, axis=0).T

    def transposed_pair(f, r):
        rows_of = (((1,), (1,)), ((), ()))
        for q in range(0, unknowns, LANES):
            width = min(LANES, unknowns - q)
            blocks = [
                raw_ref[f * NODES + b * FACE + r + each, :, q : q + width]
                for each in range(2) for b in range(NODE1)
            ]
            both = jnp.concatenate(blocks, axis=0)
            high = both.astype(jnp.bfloat16)
            low = (both - high.astype(jnp.float32)).astype(jnp.bfloat16)
            if width == LANES:
                halves = jnp.concatenate([high, low], axis=1)
                out = lax.dot_general(eye_ref[...], halves, rows_of, preferred_element_type=jnp.float32)
            else:
                eye = eye_ref[:width, :width]
                out = lax.dot_general(eye, high, rows_of, preferred_element_type=jnp.float32)
                out = out + lax.dot_general(eye, low, rows_of, preferred_element_type=jnp.float32)
            for each in range(2):
                tt_ref[f * FACE + r + each, q : q + width, :] = out[:, each * LANES : (each + 1) * LANES]

    load(0)
    load(1)

    row = lax.broadcasted_iota(jnp.int32, (SUB, LANES), 0)
    lane = lax.broadcasted_iota(jnp.int32, (SUB, LANES), 1)
    group = lane // count
    local = lane - group * count
    top = row < NODE1
    k_of = row % NODE1
    block = group[:1]

    def event(x, chunk):
        if x == 0:
            return 0
        return 1 + chunk + (min(x, 3) - 1) * len(CHUNKS)

    def copies(x, chunk):
        first, fields = chunks_of(x)[chunk]
        rows = pl.ds(first * FACE, fields * FACE)
        zrows = pl.ds(chunk * SUB, SUB)
        out = []
        for which in range(4):
            if which < 2:
                src, dst = y_ref.at[x, rows], recv_ref.at[x, which, rows]
                target = at(1) if which == 0 else at(-1)
            else:
                src, dst = zsend_ref.at[x, zrows], zrecv_ref.at[x, which - 2, zrows]
                target = at(-rotation) if which == 2 else at(-rotation - 1)
            out.append(pltpu.make_async_remote_copy(
                src_ref=src, dst_ref=dst, send_sem=send_sem.at[which // 2],
                recv_sem=recv_sem.at[event(x, chunk)], device_id={"elem": target}, device_id_type=MESH,
            ))
        return out

    def arrived(xs, chunks):
        rows = sum(2 * chunks_of(xs[0])[chunk][1] * FACE + 2 * SUB for chunk in chunks) * len(xs)
        there = tt_ref.at[0, pl.ds(0, rows)]
        pltpu.make_async_copy(there, there, recv_sem.at[event(xs[0], chunks[0])]).wait()

    def packed_rows(values, k):
        packed = jnp.zeros((SUB, LANES), jnp.float32)
        for slot, value in enumerate(values):
            shift = (slot - k) % SUB
            value = pltpu.roll(value, shift, 0) if shift else value
            packed = jnp.where(k_of == slot, value, packed)
        return packed

    def chunk_rows(x, chunk):
        first, fields = chunks_of(x)[chunk]
        return [c_rows(first + slot // 2, slot % 2) for slot in range(2 * fields)]

    def send(x, chunk):
        packed = packed_rows([y_ref[x, rows, :] for rows in chunk_rows(x, chunk)], 0)
        zsend_ref[x, chunk * SUB : (chunk + 1) * SUB, :] = packed
        out = copies(x, chunk)
        for which in (0, 1, 3, 2):
            out[which].start()

    for each in small:
        each.wait()
    uc[...] = jnp.concatenate([u_ref[...]] * SECTIONS, axis=0).T
    for f in range(FIELDS):
        for half in range(2):
            value = uc[g_rows(f, NODE1 - 1, half), :]
            for i in range(NODE1 - 2, -1, -1):
                value = jnp.where(group == i, uc[g_rows(f, i, half), :], value)
            y_ref[0, c_rows(f, half), :] = value

    for part_of in range(2, len(LOADS)):
        load(part_of)

    def found(wanted, offsets):
        index = wanted - at(offsets[0]) * count
        code = jnp.zeros_like(wanted)
        for at_code, offset in enumerate(offsets[1:]):
            here = wanted - at(offset) * count
            match = (here >= 0) & (here < count)
            index = jnp.where(match, here, index)
            code = jnp.where(match, at_code + 1, code)
        return index, code

    def beside(face):
        wanted = jnp.concatenate([nbr_ref[face : face + 1, :]] * SECTIONS, axis=1)
        return found(jnp.broadcast_to(wanted, (SUB, LANES)), (0, -1, 1))

    per_row = LANES // count
    listed = partner_ref[pl.ds(rank // per_row, 1), :]
    partner = jnp.zeros((1, LANES), jnp.int32)
    for index in range(per_row):
        part_row = jnp.concatenate([listed[:, index * count : (index + 1) * count]] * SECTIONS, axis=1)
        partner = jnp.where(rank % per_row == index, part_row, partner)
    faces = [beside(face) for face in range(5)]
    picks = [
        [
            jnp.where(group == 0, faces[0][0] + (NODE1 - 1) * count, faces[1][0]),
            jnp.where(group == 0, faces[0][1], faces[1][1]),
        ],
        [jnp.where(top, low, high) + shift for low, high, shift in zip(
            faces[2], faces[3], (group * count, 0))],
        [faces[4][0] + group * count, faces[4][1]],
    ]
    index, code = found(jnp.broadcast_to(partner, (SUB, LANES)), (rotation, rotation + 1))
    picks.append([index + group * count, code])
    for kind in range(4):
        for which in range(2):
            index_ref[kind, which] = picks[kind][which]
    def picked(kind, own, values):
        index = index_ref[kind, 0]
        code = index_ref[kind, 1]
        for at_code, value in enumerate(values):
            own = jnp.where(code == at_code + 1, take(value, index), own)
        return own

    def crossed(low, high):
        return pltpu.roll(jnp.where(top, low, high), NODE1, 0)

    def own_near(x, slot):
        for chunk, (first, fields) in enumerate(chunks_of(x)):
            for f in range(first, first + fields):
                low, high = [y_ref[x, c_rows(f, half), :] for half in range(2)]
                own_ref[slot, f, 0] = take(low, index_ref[0, 0])
                own_ref[slot, f, 1] = take(high, index_ref[0, 0])
                own_ref[slot, f, 2] = take(crossed(low, high), index_ref[1, 0])
            minus = packed_rows([y_ref[x, rows, :] for rows in chunk_rows(x, chunk)], NODE1 - 1)
            own_z[slot, chunk] = take(minus, index_ref[2, 0])

    own_near(0, 0)
    to_k_order(uc, uk)
    volume(uc, uk, lc, tk, 1.0)
    pl.semaphore_wait(barrier, len(others))
    for chunk in range(len(CHUNKS)):
        send(0, chunk)
    out_row = lax.broadcasted_iota(jnp.int32, eye_ref.shape, 0)
    out_lane = lax.broadcasted_iota(jnp.int32, eye_ref.shape, 1)
    eye_ref[...] = jnp.where(out_row == out_lane % LANES, 1.0, 0.0).astype(jnp.bfloat16)
    for f in range(FIELDS):
        loaded(f)
        for r in range(SPLIT_AT, FACE, 2):
            transposed_pair(f, r)
        for r in range(SPLIT_AT):
            transposed(f, r)

    def near_compact(x, slot, chunk):
        first, fields = chunks_of(x)[chunk]
        sides = []
        for f in range(first, first + fields):
            low, high = [
                [recv_ref[x, which, c_rows(f, half), :] for which in range(2)] for half in range(2)
            ]
            own = [own_ref[slot, f, each] for each in range(3)]
            y = picked(1, own[2], [crossed(a, b) for a, b in zip(low, high)])
            sides.append((picked(0, own[0], low), picked(0, own[1], high), y))
        there = chunk_rows(x, chunk)
        minus = [
            packed_rows([recv_ref[x, which, rows, :] for rows in there], NODE1 - 1) for which in range(2)
        ]
        plus = [zrecv_ref[x, which, chunk * SUB : (chunk + 1) * SUB, :] for which in range(2)]
        plus = picked(3, take(plus[0], index_ref[3, 0]), plus[1:])
        return sides, picked(2, own_z[slot, chunk], minus), plus

    def spread(value):
        turned = [value] + [pltpu.roll(value, i * count, 1) for i in range(1, NODE1)]
        out = []
        for i in range(NODE1):
            each = turned[(NODE1 - 1 - i) % NODE1]
            for c in range(NODE1 - 2, -1, -1):
                each = jnp.where(group == c, turned[(c - i) % NODE1], each)
            out.append(each)
        return out

    def z_state(minus, plus, slot):
        if slot:
            minus = pltpu.roll(minus, SUB - slot, 0)
        if slot != NODE1 - 1:
            plus = pltpu.roll(plus, NODE1 - 1 - slot, 0)
        return jnp.where(k_of == 0, minus, jnp.where(k_of == NODE1 - 1, plus, 0.0))

    def spread_near(x, chunk, near, put):
        sides, minus, plus = near
        minus, plus = spread(minus), spread(plus)
        first, fields = chunks_of(x)[chunk]
        for each, (x_low, x_high, y) in enumerate(sides):
            f = first + each
            for half, value in enumerate((x_low, x_high)):
                out = spread(value)
                for side, i in enumerate((0, NODE1 - 1)):
                    put(X_SLOT + 2 * side + half, f, out[i])
            out = spread(y)
            for i in range(NODE1):
                put(Y_SLOT + i, f, out[i])
                for half in range(2):
                    put(Z_SLOT + 2 * i + half, f, z_state(minus[i], plus[i], 2 * each + half))

    x_side = (group == 0) | (group == NODE1 - 1)

    def lift(x, chunk, near, v, scale=None):
        sides, minus, plus = near
        first, fields = chunks_of(x)[chunk]
        for each, (x_low, x_high, y) in enumerate(sides):
            for half, value in enumerate((x_low, x_high)):
                value = jnp.where(x_side, value, 0.0) + z_state(minus, plus, 2 * each + half)
                value = value + jnp.where(top if half == 0 else ~top, y, 0.0)
                if scale is not None:
                    value = scale * value
                out = spread(value)
                for i in range(NODE1):
                    x_ref[v, g_rows(first + each, i, half), :] = out[i]

    def folded(accs):
        for bit in (1, 2, 4):
            low = (row & bit) == 0
            accs = [
                jnp.where(low, a, pltpu.roll(b, bit, 0)) + jnp.where(low, pltpu.roll(a, SUB - bit, 0), b)
                for a, b in zip(accs[::2], accs[1::2])
            ]
        return accs[0]

    def product(t, xs, dst, fields, first, last):
        vectors = len(xs)
        accs = [[None] * SUB for _ in range(vectors)]
        if not first:
            accs = [[acc_ref[v, t, a] for a in range(SUB)] for v in range(vectors)]
        for q in range(fields[0] * SUB, (fields[0] + fields[1]) * SUB):
            rows = slice(q * SUB, (q + 1) * SUB)
            parts_of = [x[rows, :] for x in xs]
            for a in range(SUB):
                m = tt_ref[t * SUB + a, rows, :]
                for v in range(vectors):
                    term = m * parts_of[v]
                    accs[v][a] = term if accs[v][a] is None else accs[v][a] + term
        for v in range(vectors):
            if last:
                dst[v][pl.ds(pl.multiple_of(t * SUB, SUB), SUB), :] = folded(accs[v])
            else:
                for a in range(SUB):
                    acc_ref[v, t, a] = accs[v][a]

    blocks = FIELDS * FACE // SUB

    def whole(xs, dst, sends):
        for chunk, (first, fields) in enumerate(chunks_of(sends[0])):
            @pl.loop(2 * first, 2 * (first + fields))
            def _(t):
                product(t, xs, dst, (0, FIELDS), True, True)

            for x in sends:
                send(x, chunk)

    def by_chunk(source, xs, dst, sends, await_chunk, ready):
        await_chunk(0)
        ready(0)
        arriving = chunks_of(source)
        for chunk, fields in enumerate(arriving[:-1]):
            await_chunk(chunk + 1)
            ready(chunk + 1)
            for t in range(blocks):
                product(t, xs, dst, fields, chunk == 0, False)
        for chunk, (first, fields) in enumerate(chunks_of(sends[0]) if sends else [(0, FIELDS)]):
            @pl.loop(2 * first, 2 * (first + fields))
            def _(t):
                product(t, xs, dst, arriving[-1], False, True)

            for x in sends:
                send(x, chunk)

    def put_first(slot, f, value):
        near_ref[slot, f] = value

    every = range(len(CHUNKS))
    arrived([0], every)
    for chunk in every:
        spread_near(0, chunk, near_compact(0, 0, chunk), put_first)
    surface(uc, near_ref, lc, 1.0)
    whole([lc], [y_ref.at[1]], [1])
    own_near(1, 0)

    def ready_v(chunk):
        near = near_compact(1, 0, chunk)
        lift(1, chunk, near, 0)
        sides, minus, plus = near
        for each, side in enumerate(sides):
            for slot, value in enumerate(side):
                near_v[CHUNKS[chunk][0] + each, slot] = value
        near_z[chunk, 0] = minus
        near_z[chunk, 1] = plus

    by_chunk(1, [x_ref.at[0]], [y_ref.at[2]], [2], lambda chunk: arrived([1], [chunk]), ready_v)
    own_near(2, 0)

    def alpha(i):
        return time_step * sum(butcher[i])

    def coupling(i):
        return time_step * butcher[i][i] * dissipation * inv_weight

    def own(p, s):
        return p * own_sections + s % own_sections

    def per_part(value_of):
        value = jnp.float32(value_of(0))
        for other in range(1, parts):
            value = jnp.where(part == other, jnp.float32(value_of(other)), value)
        return value

    def per_lane(value_of):
        out = jnp.zeros((1, LANES), jnp.float32)
        for s in range(SECTIONS):
            out = jnp.where(block == s, per_part(lambda p, s=s: value_of(p, s)), out)
        return out

    alphas = per_lane(lambda p, s: alpha(s))
    betas = per_lane(lambda p, s: alpha(s) * coupling(s))

    for f in range(FIELDS):
        for half in range(2):
            v, w = y_ref[1, c_rows(f, half), :], y_ref[2, c_rows(f, half), :]
            for i, (v, w) in enumerate(zip(spread(v), spread(w))):
                rows = g_rows(f, i, half)
                vc[rows, :] = v
                wc[rows, :] = w
    gc[...] = uc[...] + alphas * vc[...] + betas * wc[...]
    to_k_order(gc, uk)
    volume(gc, uk, lc, tk, time_step)

    def add_v(slot, f, value):
        near_ref[slot, f] = near_ref[slot, f] + alphas * value

    def add_w(slot, f, value):
        near_ref[slot, f] = near_ref[slot, f] + betas * value

    for chunk, (first, fields) in enumerate(CHUNKS):
        sides = [[near_v[f, slot] for slot in range(3)] for f in range(first, first + fields)]
        spread_near(1, chunk, (sides, near_z[chunk, 0], near_z[chunk, 1]), add_v)
    sections = range(own_sections)
    own_alphas = [per_part(lambda p, s=s: alpha(own(p, s))) for s in sections]
    own_betas = [per_part(lambda p, s=s: alpha(own(p, s)) * coupling(own(p, s))) for s in sections]
    own_couplings = [per_part(lambda p, s=s: coupling(own(p, s))) for s in sections]
    weights = [
        [per_lane(lambda p, g, s=s, r=r: butcher[own(p, s)][(g - r) % SECTIONS]) for r in range(SECTIONS)]
        for s in sections
    ]
    for s in sections:
        x_ref[s] = -(own_alphas[s] * vc[...] + own_betas[s] * wc[...])
    for chunk in every:
        arrived([2], [chunk])
        spread_near(2, chunk, near_compact(2, 0, chunk), add_w)
    surface(gc, near_ref, lc, time_step)

    for start in range(0, unknowns, SUB):
        rows = slice(start, start + SUB)
        tend = lc[rows, :]
        turned = [tend] + [pltpu.roll(tend, r * count, 1) for r in range(1, SECTIONS)]
        for s in sections:
            total = x_ref[s, rows, :]
            for r in range(SECTIONS):
                total = total + weights[s][r] * turned[r]
            x_ref[s, rows, :] = total

    operands = [x_ref.at[s] for s in sections]
    whole(operands, [y_ref.at[3 + s] for s in sections], [3 + s for s in sections])

    def await_first(chunk):
        arrived([3 + s for s in sections], [chunk])

    def ready_first(chunk):
        for s in sections:
            lift(3 + s, chunk, near_compact(3 + s, s, chunk), s, own_couplings[s])

    for s in sections:
        own_near(3 + s, s)
    by_chunk(3, operands, [last_ref.at[s] for s in sections], [], await_first, ready_first)

    for f in range(FIELDS):
        for half in range(2):
            rows = c_rows(f, half)
            values = [
                own_alphas[s] * y_ref[1, rows, :] + own_betas[s] * y_ref[2, rows, :]
                + y_ref[3 + s, rows, :] + last_ref[s, rows, :]
                for s in sections
            ]
            values = [spread(value) for value in values]
            for i in range(NODE1):
                value = values[0][i]
                for s in sections[1:]:
                    value = jnp.where(group == s, values[s][i], value)
                gc[g_rows(f, i, half), :] = value
    rows = gc[...].T
    for s in sections:
        out_ref[s] = rows[s * count : (s + 1) * count]
    sent = sum(len(chunks_of(x)) for x in range(3 + own_sections)) * 2 * SUB
    for which, there in enumerate((recv_ref, tt_ref.at[0, pl.ds(0, sent)])):
        pltpu.make_async_copy(there, there, send_sem.at[which]).wait()


def on_device(u_start, inverses, neighbours, partners):
    count, unknowns = u_start.shape
    devices = lax.axis_size("elem")
    own_sections = SECTIONS // lax.axis_size("section")
    listed = partners.reshape(-1, LANES)
    exchanges = 3 + own_sections
    column = pltpu.VMEM((unknowns, LANES), jnp.float32)
    compact = FIELDS * FACE
    packed = len(FINE) * SUB
    change = pl.pallas_call(
        functools.partial(kernel, devices, count),
        out_shape=pltpu.VMEM((own_sections, count, unknowns), jnp.float32),
        in_specs=[pl.BlockSpec(memory_space=pl.ANY)] * 4,
        out_specs=pl.BlockSpec(memory_space=pltpu.VMEM),
        scratch_shapes=[
            pltpu.VMEM(u_start.shape, jnp.float32),
            pltpu.VMEM(neighbours.shape[::-1], jnp.int32),
            pltpu.VMEM(listed.shape, jnp.int32),
            pltpu.VMEM((unknowns, count, unknowns), jnp.float32),
            pltpu.VMEM((compact, unknowns, LANES), jnp.float32),
            pltpu.VMEM((exchanges, compact, LANES), jnp.float32),
            pltpu.VMEM((exchanges, packed, LANES), jnp.float32),
            pltpu.VMEM((exchanges, 2, compact, LANES), jnp.float32),
            pltpu.VMEM((exchanges, 2, packed, LANES), jnp.float32),
            pltpu.VMEM((4, 2, SUB, LANES), jnp.int32),
            pltpu.VMEM((FIELDS, 3, SUB, LANES), jnp.float32),
            pltpu.VMEM((len(CHUNKS), 2, SUB, LANES), jnp.float32),
            pltpu.VMEM((16, FIELDS, SUB, LANES), jnp.float32),
            pltpu.VMEM((own_sections, FIELDS, 3, SUB, LANES), jnp.float32),
            pltpu.VMEM((own_sections, len(FINE), SUB, LANES), jnp.float32),
        ]
        + [column] * 7
        + [
            pltpu.VMEM((own_sections, unknowns, LANES), jnp.float32),
            pltpu.VMEM((own_sections, compact // SUB, SUB, SUB, LANES), jnp.float32),
            pltpu.VMEM((own_sections, compact, LANES), jnp.float32),
            pltpu.VMEM((LANES, 2 * LANES), jnp.bfloat16),
            pltpu.SemaphoreType.DMA((3,)),
            pltpu.SemaphoreType.DMA((len(LOADS),)),
            pltpu.SemaphoreType.DMA((2,)),
            pltpu.SemaphoreType.DMA((1 + 2 * len(CHUNKS) + len(FINE),)),
        ],
        compiler_params=pltpu.CompilerParams(
            collective_id=0, has_side_effects=True, vmem_limit_bytes=VMEM_BYTES
        ),
    )(u_start, neighbours.T, listed, inverses)
    return u_start[None] + change


def solution(mesh):
    placed = (P("elem", None), P("elem", None, None), P("elem", None), P())
    return jax.shard_map(
        on_device, mesh=mesh, in_specs=placed, out_specs=P("section", "elem", None), check_vma=False
    )
```

```python
import functools
import math

import jax
import jax.numpy as jnp
from jax import lax
from jax.experimental import pallas as pl
from jax.experimental.pallas import tpu as pltpu
from jax.sharding import PartitionSpec as P

NODE1 = 4
SECTIONS = 4
NEWTON = 2


time_step = 0.03
dissipation = 2.0
enthalpy_factor = 3.5
radau_nodes = [0.08858795951270394, 0.4094668644407347, 0.787659461760847, 1.0]


def lobatto():
    node_count = NODE1
    inner_value = 1.0 / math.sqrt(5.0)
    lobatto_nodes = [-1.0, -inner_value, inner_value, 1.0]
    products = []
    for row in range(node_count):
        value = 1.0
        for other in range(node_count):
            if other != row:
                value = value * (lobatto_nodes[row] - lobatto_nodes[other])
        products.append(value)
    derivative = []
    for row in range(node_count):
        entries = []
        for column in range(node_count):
            if row == column:
                total = 0.0
                for other in range(node_count):
                    if other != row:
                        total = total + 1.0 / (lobatto_nodes[row] - lobatto_nodes[other])
                entries.append(2.0 * total)
            else:
                entries.append(
                    2.0
                    * (products[row] / products[column])
                    / (lobatto_nodes[row] - lobatto_nodes[column])
                )
        derivative.append(entries)
    return derivative, float(node_count * (node_count - 1) / 2.0)


def radau_table():
    section_total = SECTIONS
    butcher = []
    columns = []
    for column in range(section_total):
        coeffs = [1.0]
        scale = 1.0
        for other in range(section_total):
            if other != column:
                shifted = [0.0] + coeffs
                for position in range(len(coeffs)):
                    shifted[position] = shifted[position] - radau_nodes[other] * coeffs[position]
                coeffs = shifted
                scale = scale * (radau_nodes[column] - radau_nodes[other])
        integral = [0.0] + [
            coeffs[position] / (position + 1.0) / scale for position in range(len(coeffs))
        ]
        columns.append(integral)
    for row in range(section_total):
        entries = []
        for column in range(section_total):
            value = 0.0
            for coefficient in reversed(columns[column]):
                value = value * radau_nodes[row] + coefficient
            entries.append(value)
        butcher.append(entries)
    return butcher


FIELDS = 5
NODES = NODE1**3
FACE = NODE1**2
LANES = 128
SUB = 8
CHUNKS = ((0, 2), (2, 2), (4, 1))
FINE = tuple((f, 1) for f in range(5))
SPLIT_AT = 10
LOADS = tuple((f, 1) for f in range(5))
X_SLOT, Y_SLOT, Z_SLOT = 0, 4, 8
VMEM_BYTES = 54 * 2**20
MESH = pl.DeviceIdType.MESH


def strided(start, count):
    return pl.ds(start, count, stride=NODE1)


def to_k_order(src_ref, k_ref):
    for field in range(FIELDS):
        for k in range(NODE1):
            base = field * NODES
            k_ref[base + k * FACE : base + (k + 1) * FACE, :] = src_ref[strided(base + k, FACE), :]


def slab(src_ref, k_ref, direction, position):
    out = []
    for field in range(FIELDS):
        base = field * NODES
        if direction == 0:
            out.append(src_ref[base + position * FACE : base + (position + 1) * FACE, :])
        elif direction == 1:
            out.append(k_ref[strided(base + position, FACE), :])
        else:
            out.append(k_ref[base + position * FACE : base + (position + 1) * FACE, :])
    return out


def put_slabs(out_ref, k_ref, direction, slabs):
    for position in range(NODE1):
        for field in range(FIELDS):
            base = field * NODES
            rows = slice(base + position * FACE, base + (position + 1) * FACE)
            value = slabs[position][field]
            if direction == 0:
                out_ref[rows, :] = value
            elif direction == 1:
                k_ref[strided(base + position, FACE), :] = value
            else:
                value = k_ref[rows, :] + value
                there = strided(base + position, FACE)
                out_ref[there, :] = out_ref[there, :] + value


def speed2(state):
    return state[1] * state[1] + state[2] * state[2] + state[3] * state[3]


def two_point(a, ka, b, kb, direction):
    r = a[0] + b[0]
    v = [a[1 + c] + b[1 + c] for c in range(3)]
    p = a[4] + b[4]
    n = v[direction]
    m = (0.25 * r) * n
    half = 0.5 * m
    out = [m]
    for c in range(3):
        term = half * v[c]
        if c == direction:
            term = term + 0.5 * p
        out.append(term)
    out.append((0.25 * enthalpy_factor * p) * n + (0.5 * half) * (ka + kb))
    return out


def volume(uc, uk, out_ref, tk, scale):
    deriv, _ = lobatto()
    for direction in range(3):
        states = [slab(uc, uk, direction, pos) for pos in range(NODE1)]
        speeds = [speed2(state) for state in states]
        sums = [None] * NODE1
        for a in range(NODE1):
            for b in range(a + 1, NODE1):
                f = two_point(states[a], speeds[a], states[b], speeds[b], direction)
                for at, other in ((a, b), (b, a)):
                    c = -2.0 * scale * deriv[at][other]
                    terms = [c * x for x in f]
                    sums[at] = terms if sums[at] is None else [x + y for x, y in zip(sums[at], terms)]
        put_slabs(out_ref, tk, direction, sums)


def face_terms(own, other, direction, flux_scale, jump_scale):
    f = two_point(own, speed2(own), other, speed2(other), direction)
    return [flux_scale * x - jump_scale * (n - u) for x, n, u in zip(f, other, own)]


def surface(g, near_ref, out_ref, scale):
    _, inv_weight = lobatto()
    c = -2.0 * scale * inv_weight
    d = 0.5 * dissipation * c
    row = lax.broadcasted_iota(jnp.int32, (SUB, LANES), 0)
    top = row < NODE1
    k = row % NODE1
    y_scale = jnp.where(top, -c, c)
    z_scale = jnp.where(k == 0, -c, jnp.where(k == NODE1 - 1, c, 0.0))
    z_jump = jnp.where((k == 0) | (k == NODE1 - 1), d, 0.0)

    for i in range(NODE1):
        rows = [[g_rows(f, i, half) for f in range(FIELDS)] for half in range(2)]
        own = [[g[rows[half][f], :] for f in range(FIELDS)] for half in range(2)]
        total = [
            face_terms(own[half], near_state(near_ref, Z_SLOT + 2 * i + half), 2, z_scale, z_jump)
            for half in range(2)
        ]
        y_own = [jnp.where(top, low, high) for low, high in zip(*own)]
        y_terms = face_terms(y_own, near_state(near_ref, Y_SLOT + i), 1, y_scale, d)
        total = [
            [t + jnp.where(top if half == 0 else ~top, y, 0.0) for t, y in zip(total[half], y_terms)]
            for half in range(2)
        ]
        if i in (0, NODE1 - 1):
            side = 0 if i == 0 else 1
            for half in range(2):
                x_terms = face_terms(
                    own[half], near_state(near_ref, X_SLOT + 2 * side + half), 0, (2 * side - 1) * c, d
                )
                total[half] = [t + x for t, x in zip(total[half], x_terms)]
        for half in range(2):
            for f in range(FIELDS):
                out_ref[rows[half][f], :] = out_ref[rows[half][f], :] + total[half][f]


def g_rows(f, i, half):
    start = f * NODES + i * FACE + half * SUB
    return slice(start, start + SUB)


def c_rows(f, half):
    start = f * FACE + half * SUB
    return slice(start, start + SUB)


def chunks_of(x):
    return CHUNKS if x in (0, 2) else FINE


def near_state(near_ref, slot):
    return [near_ref[slot, f] for f in range(FIELDS)]


def take(value, index):
    return jnp.take_along_axis(value, index, axis=1, mode="promise_in_bounds")


def kernel(
    devices, count, u_in, nbr_in, partner_in, inv_ref, out_ref,
    u_ref, nbr_ref, partner_ref,
    raw_ref, tt_ref, y_ref, zsend_ref, recv_ref, zrecv_ref, index_ref, near_v, near_z, near_ref, own_ref, own_z,
    uc, uk, vc, wc, lc, tk, gc, x_ref, acc_ref, last_ref, eye_ref,
    in_sem, a_sem, send_sem, recv_sem,
):
    rank = lax.axis_index("elem")
    part = lax.axis_index("section")
    parts = lax.axis_size("section")
    own_sections = SECTIONS // parts
    rotation = devices // 4
    unknowns = FIELDS * NODES
    butcher = radau_table()
    _, inv_weight = lobatto()

    def at(offset):
        return lax.rem(rank + (offset + devices), devices)

    def load(part_of):
        first, fields = LOADS[part_of]
        rows = pl.ds(first * NODES, fields * NODES)
        for e in range(count):
            pltpu.make_async_copy(inv_ref.at[e, rows], raw_ref.at[rows, e], a_sem.at[part_of]).start()

    small = [
        pltpu.make_async_copy(src, dst, in_sem.at[index])
        for index, (src, dst) in enumerate(
            ((u_in, u_ref), (nbr_in, nbr_ref), (partner_in, partner_ref))
        )
    ]
    for each in small:
        each.start()
    barrier = pltpu.get_barrier_semaphore()
    others = (1, -1, rotation, -rotation, rotation + 1, -rotation - 1)
    for offset in others:
        pl.semaphore_signal(barrier, inc=1, device_id={"elem": at(offset)}, device_id_type=MESH)
    def loaded(part_of):
        first, fields = LOADS[part_of]
        there = raw_ref.at[pl.ds(first * NODES, fields * NODES)]
        pltpu.make_async_copy(there, there, a_sem.at[part_of]).wait()

    def transposed(f, r):
        for q in range(0, unknowns, LANES):
            width = min(LANES, unknowns - q)
            blocks = [raw_ref[f * NODES + b * FACE + r, :, q : q + width] for b in range(NODE1)]
            tt_ref[f * FACE + r, q : q + width, :] = jnp.concatenate(blocks, axis=0).T

    def transposed_pair(f, r):
        rows_of = (((1,), (1,)), ((), ()))
        for q in range(0, unknowns, LANES):
            width = min(LANES, unknowns - q)
            blocks = [
                raw_ref[f * NODES + b * FACE + r + each, :, q : q + width]
                for each in range(2) for b in range(NODE1)
            ]
            both = jnp.concatenate(blocks, axis=0)
            high = both.astype(jnp.bfloat16)
            low = (both - high.astype(jnp.float32)).astype(jnp.bfloat16)
            if width == LANES:
                halves = jnp.concatenate([high, low], axis=1)
                out = lax.dot_general(eye_ref[...], halves, rows_of, preferred_element_type=jnp.float32)
            else:
                eye = eye_ref[:width, :width]
                out = lax.dot_general(eye, high, rows_of, preferred_element_type=jnp.float32)
                out = out + lax.dot_general(eye, low, rows_of, preferred_element_type=jnp.float32)
            for each in range(2):
                tt_ref[f * FACE + r + each, q : q + width, :] = out[:, each * LANES : (each + 1) * LANES]

    for part_of in range(len(LOADS)):
        load(part_of)

    row = lax.broadcasted_iota(jnp.int32, (SUB, LANES), 0)
    lane = lax.broadcasted_iota(jnp.int32, (SUB, LANES), 1)
    group = lane // count
    local = lane - group * count
    top = row < NODE1
    k_of = row % NODE1
    block = group[:1]

    def event(x, chunk):
        if x == 0:
            return 0
        return 1 + chunk + sum(len(chunks_of(each)) for each in range(1, min(x, 3)))

    def copies(x, chunk):
        first, fields = chunks_of(x)[chunk]
        rows = pl.ds(first * FACE, fields * FACE)
        zrows = pl.ds(chunk * SUB, SUB)
        out = []
        for which in range(4):
            if which < 2:
                src, dst = y_ref.at[x, rows], recv_ref.at[x, which, rows]
                target = at(1) if which == 0 else at(-1)
            else:
                src, dst = zsend_ref.at[x, zrows], zrecv_ref.at[x, which - 2, zrows]
                target = at(-rotation) if which == 2 else at(-rotation - 1)
            out.append(pltpu.make_async_remote_copy(
                src_ref=src, dst_ref=dst, send_sem=send_sem.at[which // 2],
                recv_sem=recv_sem.at[event(x, chunk)], device_id={"elem": target}, device_id_type=MESH,
            ))
        return out

    def arrived(xs, chunks):
        rows = sum(2 * chunks_of(xs[0])[chunk][1] * FACE + 2 * SUB for chunk in chunks) * len(xs)
        there = tt_ref.at[0, pl.ds(0, rows)]
        pltpu.make_async_copy(there, there, recv_sem.at[event(xs[0], chunks[0])]).wait()

    def packed_rows(values, k):
        packed = jnp.zeros((SUB, LANES), jnp.float32)
        for slot, value in enumerate(values):
            shift = (slot - k) % SUB
            value = pltpu.roll(value, shift, 0) if shift else value
            packed = jnp.where(k_of == slot, value, packed)
        return packed

    def chunk_rows(x, chunk):
        first, fields = chunks_of(x)[chunk]
        return [c_rows(first + slot // 2, slot % 2) for slot in range(2 * fields)]

    def send(x, chunk):
        packed = packed_rows([y_ref[x, rows, :] for rows in chunk_rows(x, chunk)], 0)
        zsend_ref[x, chunk * SUB : (chunk + 1) * SUB, :] = packed
        out = copies(x, chunk)
        for which in (0, 1, 3, 2):
            out[which].start()

    for each in small:
        each.wait()
    uc[...] = jnp.concatenate([u_ref[...]] * SECTIONS, axis=0).T
    for f in range(FIELDS):
        for half in range(2):
            value = uc[g_rows(f, NODE1 - 1, half), :]
            for i in range(NODE1 - 2, -1, -1):
                value = jnp.where(group == i, uc[g_rows(f, i, half), :], value)
            y_ref[0, c_rows(f, half), :] = value

    to_k_order(uc, uk)
    volume(uc, uk, lc, tk, 1.0)
    pl.semaphore_wait(barrier, len(others))
    for chunk in range(len(CHUNKS)):
        send(0, chunk)

    def found(wanted, offsets):
        index = wanted - at(offsets[0]) * count
        code = jnp.zeros_like(wanted)
        for at_code, offset in enumerate(offsets[1:]):
            here = wanted - at(offset) * count
            match = (here >= 0) & (here < count)
            index = jnp.where(match, here, index)
            code = jnp.where(match, at_code + 1, code)
        return index, code

    def beside(face):
        wanted = jnp.concatenate([nbr_ref[face : face + 1, :]] * SECTIONS, axis=1)
        return found(jnp.broadcast_to(wanted, (SUB, LANES)), (0, -1, 1))

    per_row = LANES // count
    listed = partner_ref[pl.ds(rank // per_row, 1), :]
    partner = jnp.zeros((1, LANES), jnp.int32)
    for index in range(per_row):
        part_row = jnp.concatenate([listed[:, index * count : (index + 1) * count]] * SECTIONS, axis=1)
        partner = jnp.where(rank % per_row == index, part_row, partner)
    faces = [beside(face) for face in range(5)]
    picks = [
        [
            jnp.where(group == 0, faces[0][0] + (NODE1 - 1) * count, faces[1][0]),
            jnp.where(group == 0, faces[0][1], faces[1][1]),
        ],
        [jnp.where(top, low, high) + shift for low, high, shift in zip(
            faces[2], faces[3], (group * count, 0))],
        [faces[4][0] + group * count, faces[4][1]],
    ]
    index, code = found(jnp.broadcast_to(partner, (SUB, LANES)), (rotation, rotation + 1))
    picks.append([index + group * count, code])
    for kind in range(4):
        for which in range(2):
            index_ref[kind, which] = picks[kind][which]
    def picked(kind, own, values):
        index = index_ref[kind, 0]
        code = index_ref[kind, 1]
        for at_code, value in enumerate(values):
            own = jnp.where(code == at_code + 1, take(value, index), own)
        return own

    def crossed(low, high):
        return pltpu.roll(jnp.where(top, low, high), NODE1, 0)

    def own_near(x, slot):
        for chunk, (first, fields) in enumerate(chunks_of(x)):
            for f in range(first, first + fields):
                low, high = [y_ref[x, c_rows(f, half), :] for half in range(2)]
                own_ref[slot, f, 0] = take(low, index_ref[0, 0])
                own_ref[slot, f, 1] = take(high, index_ref[0, 0])
                own_ref[slot, f, 2] = take(crossed(low, high), index_ref[1, 0])
            minus = packed_rows([y_ref[x, rows, :] for rows in chunk_rows(x, chunk)], NODE1 - 1)
            own_z[slot, chunk] = take(minus, index_ref[2, 0])

    own_near(0, 0)
    out_row = lax.broadcasted_iota(jnp.int32, eye_ref.shape, 0)
    out_lane = lax.broadcasted_iota(jnp.int32, eye_ref.shape, 1)
    eye_ref[...] = jnp.where(out_row == out_lane % LANES, 1.0, 0.0).astype(jnp.bfloat16)
    for f in range(FIELDS):
        loaded(f)
        for r in range(SPLIT_AT, FACE, 2):
            transposed_pair(f, r)
        for r in range(SPLIT_AT):
            transposed(f, r)

    def near_compact(x, slot, chunk):
        first, fields = chunks_of(x)[chunk]
        sides = []
        for f in range(first, first + fields):
            low, high = [
                [recv_ref[x, which, c_rows(f, half), :] for which in range(2)] for half in range(2)
            ]
            own = [own_ref[slot, f, each] for each in range(3)]
            y = picked(1, own[2], [crossed(a, b) for a, b in zip(low, high)])
            sides.append((picked(0, own[0], low), picked(0, own[1], high), y))
        there = chunk_rows(x, chunk)
        minus = [
            packed_rows([recv_ref[x, which, rows, :] for rows in there], NODE1 - 1) for which in range(2)
        ]
        plus = [zrecv_ref[x, which, chunk * SUB : (chunk + 1) * SUB, :] for which in range(2)]
        plus = picked(3, take(plus[0], index_ref[3, 0]), plus[1:])
        return sides, picked(2, own_z[slot, chunk], minus), plus

    def spread(value):
        turned = [value] + [pltpu.roll(value, i * count, 1) for i in range(1, NODE1)]
        out = []
        for i in range(NODE1):
            each = turned[(NODE1 - 1 - i) % NODE1]
            for c in range(NODE1 - 2, -1, -1):
                each = jnp.where(group == c, turned[(c - i) % NODE1], each)
            out.append(each)
        return out

    def z_state(minus, plus, slot):
        if slot:
            minus = pltpu.roll(minus, SUB - slot, 0)
        if slot != NODE1 - 1:
            plus = pltpu.roll(plus, NODE1 - 1 - slot, 0)
        return jnp.where(k_of == 0, minus, jnp.where(k_of == NODE1 - 1, plus, 0.0))

    def spread_near(x, chunk, near, put):
        sides, minus, plus = near
        minus, plus = spread(minus), spread(plus)
        first, fields = chunks_of(x)[chunk]
        for each, (x_low, x_high, y) in enumerate(sides):
            f = first + each
            for half, value in enumerate((x_low, x_high)):
                out = spread(value)
                for side, i in enumerate((0, NODE1 - 1)):
                    put(X_SLOT + 2 * side + half, f, out[i])
            out = spread(y)
            for i in range(NODE1):
                put(Y_SLOT + i, f, out[i])
                for half in range(2):
                    put(Z_SLOT + 2 * i + half, f, z_state(minus[i], plus[i], 2 * each + half))

    x_side = (group == 0) | (group == NODE1 - 1)

    def lift(x, chunk, near, v, scale=None):
        sides, minus, plus = near
        first, fields = chunks_of(x)[chunk]
        for each, (x_low, x_high, y) in enumerate(sides):
            for half, value in enumerate((x_low, x_high)):
                value = jnp.where(x_side, value, 0.0) + z_state(minus, plus, 2 * each + half)
                value = value + jnp.where(top if half == 0 else ~top, y, 0.0)
                if scale is not None:
                    value = scale * value
                out = spread(value)
                for i in range(NODE1):
                    x_ref[v, g_rows(first + each, i, half), :] = out[i]

    def folded(accs):
        for bit in (1, 2, 4):
            low = (row & bit) == 0
            accs = [
                jnp.where(low, a, pltpu.roll(b, bit, 0)) + jnp.where(low, pltpu.roll(a, SUB - bit, 0), b)
                for a, b in zip(accs[::2], accs[1::2])
            ]
        return accs[0]

    def product(t, xs, dst, fields, first, last):
        vectors = len(xs)
        accs = [[None] * SUB for _ in range(vectors)]
        if not first:
            accs = [[acc_ref[v, t, a] for a in range(SUB)] for v in range(vectors)]
        for q in range(fields[0] * SUB, (fields[0] + fields[1]) * SUB):
            rows = slice(q * SUB, (q + 1) * SUB)
            parts_of = [x[rows, :] for x in xs]
            for a in range(SUB):
                m = tt_ref[t * SUB + a, rows, :]
                for v in range(vectors):
                    term = m * parts_of[v]
                    accs[v][a] = term if accs[v][a] is None else accs[v][a] + term
        for v in range(vectors):
            if last:
                dst[v][t * SUB : (t + 1) * SUB, :] = folded(accs[v])
            else:
                for a in range(SUB):
                    acc_ref[v, t, a] = accs[v][a]

    blocks = FIELDS * FACE // SUB

    def whole(xs, dst, sends):
        for chunk, (first, fields) in enumerate(chunks_of(sends[0])):
            for t in range(2 * first, 2 * (first + fields)):
                product(t, xs, dst, (0, FIELDS), True, True)
            for x in sends:
                send(x, chunk)

    def by_chunk(source, xs, dst, sends, await_chunk, ready):
        await_chunk(0)
        ready(0)
        arriving = chunks_of(source)
        for chunk, fields in enumerate(arriving[:-1]):
            await_chunk(chunk + 1)
            ready(chunk + 1)
            for t in range(blocks):
                product(t, xs, dst, fields, chunk == 0, False)
        for chunk, (first, fields) in enumerate(chunks_of(sends[0]) if sends else [(0, FIELDS)]):
            for t in range(2 * first, 2 * (first + fields)):
                product(t, xs, dst, arriving[-1], False, True)
            for x in sends:
                send(x, chunk)

    def put_first(slot, f, value):
        near_ref[slot, f] = value

    every = range(len(CHUNKS))
    arrived([0], every)
    for chunk in every:
        spread_near(0, chunk, near_compact(0, 0, chunk), put_first)
    surface(uc, near_ref, lc, 1.0)
    whole([lc], [y_ref.at[1]], [1])
    own_near(1, 0)

    def ready_v(chunk):
        near = near_compact(1, 0, chunk)
        lift(1, chunk, near, 0)
        sides, minus, plus = near
        for each, side in enumerate(sides):
            for slot, value in enumerate(side):
                near_v[chunks_of(1)[chunk][0] + each, slot] = value
        near_z[chunk, 0] = minus
        near_z[chunk, 1] = plus

    by_chunk(1, [x_ref.at[0]], [y_ref.at[2]], [2], lambda chunk: arrived([1], [chunk]), ready_v)
    own_near(2, 0)

    def alpha(i):
        return time_step * sum(butcher[i])

    def coupling(i):
        return time_step * butcher[i][i] * dissipation * inv_weight

    def own(p, s):
        return p * own_sections + s % own_sections

    def per_part(value_of):
        value = jnp.float32(value_of(0))
        for other in range(1, parts):
            value = jnp.where(part == other, jnp.float32(value_of(other)), value)
        return value

    def per_lane(value_of):
        out = jnp.zeros((1, LANES), jnp.float32)
        for s in range(SECTIONS):
            out = jnp.where(block == s, per_part(lambda p, s=s: value_of(p, s)), out)
        return out

    alphas = per_lane(lambda p, s: alpha(s))
    betas = per_lane(lambda p, s: alpha(s) * coupling(s))

    for f in range(FIELDS):
        for half in range(2):
            v, w = y_ref[1, c_rows(f, half), :], y_ref[2, c_rows(f, half), :]
            for i, (v, w) in enumerate(zip(spread(v), spread(w))):
                rows = g_rows(f, i, half)
                vc[rows, :] = v
                wc[rows, :] = w
    gc[...] = uc[...] + alphas * vc[...] + betas * wc[...]
    to_k_order(gc, uk)
    volume(gc, uk, lc, tk, time_step)

    def add_v(slot, f, value):
        near_ref[slot, f] = near_ref[slot, f] + alphas * value

    def add_w(slot, f, value):
        near_ref[slot, f] = near_ref[slot, f] + betas * value

    for chunk, (first, fields) in enumerate(chunks_of(1)):
        sides = [[near_v[f, slot] for slot in range(3)] for f in range(first, first + fields)]
        spread_near(1, chunk, (sides, near_z[chunk, 0], near_z[chunk, 1]), add_v)
    sections = range(own_sections)
    own_alphas = [per_part(lambda p, s=s: alpha(own(p, s))) for s in sections]
    own_betas = [per_part(lambda p, s=s: alpha(own(p, s)) * coupling(own(p, s))) for s in sections]
    own_couplings = [per_part(lambda p, s=s: coupling(own(p, s))) for s in sections]
    weights = [
        [per_lane(lambda p, g, s=s, r=r: butcher[own(p, s)][(g - r) % SECTIONS]) for r in range(SECTIONS)]
        for s in sections
    ]
    for s in sections:
        x_ref[s] = -(own_alphas[s] * vc[...] + own_betas[s] * wc[...])
    for chunk in every:
        arrived([2], [chunk])
        spread_near(2, chunk, near_compact(2, 0, chunk), add_w)
    surface(gc, near_ref, lc, time_step)

    for start in range(0, unknowns, SUB):
        rows = slice(start, start + SUB)
        tend = lc[rows, :]
        turned = [tend] + [pltpu.roll(tend, r * count, 1) for r in range(1, SECTIONS)]
        for s in sections:
            total = x_ref[s, rows, :]
            for r in range(SECTIONS):
                total = total + weights[s][r] * turned[r]
            x_ref[s, rows, :] = total

    operands = [x_ref.at[s] for s in sections]
    whole(operands, [y_ref.at[3 + s] for s in sections], [3 + s for s in sections])

    def await_first(chunk):
        arrived([3 + s for s in sections], [chunk])

    def ready_first(chunk):
        for s in sections:
            lift(3 + s, chunk, near_compact(3 + s, s, chunk), s, own_couplings[s])

    for s in sections:
        own_near(3 + s, s)
    by_chunk(3, operands, [last_ref.at[s] for s in sections], [], await_first, ready_first)

    for f in range(FIELDS):
        for half in range(2):
            rows = c_rows(f, half)
            values = [
                own_alphas[s] * y_ref[1, rows, :] + own_betas[s] * y_ref[2, rows, :]
                + y_ref[3 + s, rows, :] + last_ref[s, rows, :]
                for s in sections
            ]
            values = [spread(value) for value in values]
            for i in range(NODE1):
                value = values[0][i]
                for s in sections[1:]:
                    value = jnp.where(group == s, values[s][i], value)
                gc[g_rows(f, i, half), :] = value
    rows = gc[...].T
    for s in sections:
        out_ref[s] = rows[s * count : (s + 1) * count]
    sent = sum(len(chunks_of(x)) for x in range(3 + own_sections)) * 2 * SUB
    for which, there in enumerate((recv_ref, tt_ref.at[pl.ds(0, 2), pl.ds(0, sent // 2)])):
        pltpu.make_async_copy(there, there, send_sem.at[which]).wait()


def on_device(u_start, inverses, neighbours, partners):
    count, unknowns = u_start.shape
    devices = lax.axis_size("elem")
    own_sections = SECTIONS // lax.axis_size("section")
    listed = partners.reshape(-1, LANES)
    exchanges = 3 + own_sections
    column = pltpu.VMEM((unknowns, LANES), jnp.float32)
    compact = FIELDS * FACE
    packed = len(FINE) * SUB
    change = pl.pallas_call(
        functools.partial(kernel, devices, count),
        out_shape=pltpu.VMEM((own_sections, count, unknowns), jnp.float32),
        in_specs=[pl.BlockSpec(memory_space=pl.ANY)] * 4,
        out_specs=pl.BlockSpec(memory_space=pltpu.VMEM),
        scratch_shapes=[
            pltpu.VMEM(u_start.shape, jnp.float32),
            pltpu.VMEM(neighbours.shape[::-1], jnp.int32),
            pltpu.VMEM(listed.shape, jnp.int32),
            pltpu.VMEM((unknowns, count, unknowns), jnp.float32),
            pltpu.VMEM((compact, unknowns, LANES), jnp.float32),
            pltpu.VMEM((exchanges, compact, LANES), jnp.float32),
            pltpu.VMEM((exchanges, packed, LANES), jnp.float32),
            pltpu.VMEM((exchanges, 2, compact, LANES), jnp.float32),
            pltpu.VMEM((exchanges, 2, packed, LANES), jnp.float32),
            pltpu.VMEM((4, 2, SUB, LANES), jnp.int32),
            pltpu.VMEM((FIELDS, 3, SUB, LANES), jnp.float32),
            pltpu.VMEM((len(FINE), 2, SUB, LANES), jnp.float32),
            pltpu.VMEM((16, FIELDS, SUB, LANES), jnp.float32),
            pltpu.VMEM((own_sections, FIELDS, 3, SUB, LANES), jnp.float32),
            pltpu.VMEM((own_sections, len(FINE), SUB, LANES), jnp.float32),
        ]
        + [column] * 7
        + [
            pltpu.VMEM((own_sections, unknowns, LANES), jnp.float32),
            pltpu.VMEM((own_sections, compact // SUB, SUB, SUB, LANES), jnp.float32),
            pltpu.VMEM((own_sections, compact, LANES), jnp.float32),
            pltpu.VMEM((LANES, 2 * LANES), jnp.bfloat16),
            pltpu.SemaphoreType.DMA((3,)),
            pltpu.SemaphoreType.DMA((len(LOADS),)),
            pltpu.SemaphoreType.DMA((2,)),
            pltpu.SemaphoreType.DMA((1 + len(CHUNKS) + 2 * len(FINE),)),
        ],
        compiler_params=pltpu.CompilerParams(
            collective_id=0, has_side_effects=True, vmem_limit_bytes=VMEM_BYTES
        ),
    )(u_start, neighbours.T, listed, inverses)
    return u_start[None] + change


def solution(mesh):
    placed = (P("elem", None), P("elem", None, None), P("elem", None), P())
    return jax.shard_map(
        on_device, mesh=mesh, in_specs=placed, out_specs=P("section", "elem", None), check_vma=False
    )
```

```python
import functools
import math

import jax
import jax.numpy as jnp
from jax import lax
from jax.experimental import pallas as pl
from jax.experimental.pallas import tpu as pltpu
from jax.sharding import PartitionSpec as P

NODE1 = 4
SECTIONS = 4
NEWTON = 2


time_step = 0.03
dissipation = 2.0
enthalpy_factor = 3.5
radau_nodes = [0.08858795951270394, 0.4094668644407347, 0.787659461760847, 1.0]


def lobatto():
    node_count = NODE1
    inner_value = 1.0 / math.sqrt(5.0)
    lobatto_nodes = [-1.0, -inner_value, inner_value, 1.0]
    products = []
    for row in range(node_count):
        value = 1.0
        for other in range(node_count):
            if other != row:
                value = value * (lobatto_nodes[row] - lobatto_nodes[other])
        products.append(value)
    derivative = []
    for row in range(node_count):
        entries = []
        for column in range(node_count):
            if row == column:
                total = 0.0
                for other in range(node_count):
                    if other != row:
                        total = total + 1.0 / (lobatto_nodes[row] - lobatto_nodes[other])
                entries.append(2.0 * total)
            else:
                entries.append(
                    2.0
                    * (products[row] / products[column])
                    / (lobatto_nodes[row] - lobatto_nodes[column])
                )
        derivative.append(entries)
    return derivative, float(node_count * (node_count - 1) / 2.0)


def radau_table():
    section_total = SECTIONS
    butcher = []
    columns = []
    for column in range(section_total):
        coeffs = [1.0]
        scale = 1.0
        for other in range(section_total):
            if other != column:
                shifted = [0.0] + coeffs
                for position in range(len(coeffs)):
                    shifted[position] = shifted[position] - radau_nodes[other] * coeffs[position]
                coeffs = shifted
                scale = scale * (radau_nodes[column] - radau_nodes[other])
        integral = [0.0] + [
            coeffs[position] / (position + 1.0) / scale for position in range(len(coeffs))
        ]
        columns.append(integral)
    for row in range(section_total):
        entries = []
        for column in range(section_total):
            value = 0.0
            for coefficient in reversed(columns[column]):
                value = value * radau_nodes[row] + coefficient
            entries.append(value)
        butcher.append(entries)
    return butcher


FIELDS = 5
NODES = NODE1**3
FACE = NODE1**2
LANES = 128
SUB = 8
CHUNKS = ((0, 2), (2, 2), (4, 1))
FINE = tuple((f, 1) for f in range(5))
SPLIT_AT = 10
LOADS = tuple((f, 1) for f in range(5))
X_SLOT, Y_SLOT, Z_SLOT = 0, 4, 8
VMEM_BYTES = 54 * 2**20
MESH = pl.DeviceIdType.MESH


def strided(start, count):
    return pl.ds(start, count, stride=NODE1)


def to_k_order(src_ref, k_ref):
    for field in range(FIELDS):
        for k in range(NODE1):
            base = field * NODES
            k_ref[base + k * FACE : base + (k + 1) * FACE, :] = src_ref[strided(base + k, FACE), :]


def slab(src_ref, k_ref, direction, position):
    out = []
    for field in range(FIELDS):
        base = field * NODES
        if direction == 0:
            out.append(src_ref[base + position * FACE : base + (position + 1) * FACE, :])
        elif direction == 1:
            out.append(k_ref[strided(base + position, FACE), :])
        else:
            out.append(k_ref[base + position * FACE : base + (position + 1) * FACE, :])
    return out


def put_slabs(out_ref, k_ref, direction, slabs):
    for position in range(NODE1):
        for field in range(FIELDS):
            base = field * NODES
            rows = slice(base + position * FACE, base + (position + 1) * FACE)
            value = slabs[position][field]
            if direction == 0:
                out_ref[rows, :] = value
            elif direction == 1:
                k_ref[strided(base + position, FACE), :] = value
            else:
                value = k_ref[rows, :] + value
                there = strided(base + position, FACE)
                out_ref[there, :] = out_ref[there, :] + value


def speed2(state):
    return state[1] * state[1] + state[2] * state[2] + state[3] * state[3]


def two_point(a, ka, b, kb, direction):
    r = a[0] + b[0]
    v = [a[1 + c] + b[1 + c] for c in range(3)]
    p = a[4] + b[4]
    n = v[direction]
    m = (0.25 * r) * n
    half = 0.5 * m
    out = [m]
    for c in range(3):
        term = half * v[c]
        if c == direction:
            term = term + 0.5 * p
        out.append(term)
    out.append((0.25 * enthalpy_factor * p) * n + (0.5 * half) * (ka + kb))
    return out


def volume(uc, uk, out_ref, tk, scale):
    deriv, _ = lobatto()
    for direction in range(3):
        states = [slab(uc, uk, direction, pos) for pos in range(NODE1)]
        speeds = [speed2(state) for state in states]
        sums = [None] * NODE1
        for a in range(NODE1):
            for b in range(a + 1, NODE1):
                f = two_point(states[a], speeds[a], states[b], speeds[b], direction)
                for at, other in ((a, b), (b, a)):
                    c = -2.0 * scale * deriv[at][other]
                    terms = [c * x for x in f]
                    sums[at] = terms if sums[at] is None else [x + y for x, y in zip(sums[at], terms)]
        put_slabs(out_ref, tk, direction, sums)


def face_terms(own, other, direction, flux_scale, jump_scale):
    f = two_point(own, speed2(own), other, speed2(other), direction)
    return [flux_scale * x - jump_scale * (n - u) for x, n, u in zip(f, other, own)]


def surface(g, near_ref, out_ref, scale):
    _, inv_weight = lobatto()
    c = -2.0 * scale * inv_weight
    d = 0.5 * dissipation * c
    row = lax.broadcasted_iota(jnp.int32, (SUB, LANES), 0)
    top = row < NODE1
    k = row % NODE1
    y_scale = jnp.where(top, -c, c)
    z_scale = jnp.where(k == 0, -c, jnp.where(k == NODE1 - 1, c, 0.0))
    z_jump = jnp.where((k == 0) | (k == NODE1 - 1), d, 0.0)

    for i in range(NODE1):
        rows = [[g_rows(f, i, half) for f in range(FIELDS)] for half in range(2)]
        own = [[g[rows[half][f], :] for f in range(FIELDS)] for half in range(2)]
        total = [
            face_terms(own[half], near_state(near_ref, Z_SLOT + 2 * i + half), 2, z_scale, z_jump)
            for half in range(2)
        ]
        y_own = [jnp.where(top, low, high) for low, high in zip(*own)]
        y_terms = face_terms(y_own, near_state(near_ref, Y_SLOT + i), 1, y_scale, d)
        total = [
            [t + jnp.where(top if half == 0 else ~top, y, 0.0) for t, y in zip(total[half], y_terms)]
            for half in range(2)
        ]
        if i in (0, NODE1 - 1):
            side = 0 if i == 0 else 1
            for half in range(2):
                x_terms = face_terms(
                    own[half], near_state(near_ref, X_SLOT + 2 * side + half), 0, (2 * side - 1) * c, d
                )
                total[half] = [t + x for t, x in zip(total[half], x_terms)]
        for half in range(2):
            for f in range(FIELDS):
                out_ref[rows[half][f], :] = out_ref[rows[half][f], :] + total[half][f]


def g_rows(f, i, half):
    start = f * NODES + i * FACE + half * SUB
    return slice(start, start + SUB)


def c_rows(f, half):
    start = f * FACE + half * SUB
    return slice(start, start + SUB)


def chunks_of(x):
    return CHUNKS if x in (0, 2) else FINE


def near_state(near_ref, slot):
    return [near_ref[slot, f] for f in range(FIELDS)]


def take(value, index):
    return jnp.take_along_axis(value, index, axis=1, mode="promise_in_bounds")


def kernel(
    devices, count, u_in, nbr_in, partner_in, inv_ref, out_ref,
    u_ref, nbr_ref, partner_ref,
    raw_ref, tt_ref, y_ref, zsend_ref, recv_ref, zrecv_ref, index_ref, near_v, near_z, near_ref, own_ref, own_z,
    uc, uk, vc, wc, lc, tk, gc, x_ref, acc_ref, last_ref, eye_ref,
    in_sem, a_sem, send_sem, recv_sem,
):
    rank = lax.axis_index("elem")
    part = lax.axis_index("section")
    parts = lax.axis_size("section")
    own_sections = SECTIONS // parts
    rotation = devices // 4
    unknowns = FIELDS * NODES
    butcher = radau_table()
    _, inv_weight = lobatto()

    def at(offset):
        return lax.rem(rank + (offset + devices), devices)

    def load(part_of):
        first, fields = LOADS[part_of]
        rows = pl.ds(first * NODES, fields * NODES)
        for e in range(count):
            pltpu.make_async_copy(inv_ref.at[e, rows], raw_ref.at[rows, e], a_sem.at[part_of]).start()

    small = [
        pltpu.make_async_copy(src, dst, in_sem.at[index])
        for index, (src, dst) in enumerate(
            ((u_in, u_ref), (nbr_in, nbr_ref), (partner_in, partner_ref))
        )
    ]
    for each in small:
        each.start()
    barrier = pltpu.get_barrier_semaphore()
    others = (1, -1, rotation, -rotation, rotation + 1, -rotation - 1)
    for offset in others:
        pl.semaphore_signal(barrier, inc=1, device_id={"elem": at(offset)}, device_id_type=MESH)
    def loaded(part_of):
        first, fields = LOADS[part_of]
        there = raw_ref.at[pl.ds(first * NODES, fields * NODES)]
        pltpu.make_async_copy(there, there, a_sem.at[part_of]).wait()

    def transposed(f, r):
        for q in range(0, unknowns, LANES):
            width = min(LANES, unknowns - q)
            blocks = [raw_ref[f * NODES + b * FACE + r, :, q : q + width] for b in range(NODE1)]
            tt_ref[f * FACE + r, q : q + width, :] = jnp.concatenate(blocks, axis=0).T

    def transposed_pair(f, r):
        rows_of = (((1,), (1,)), ((), ()))
        for q in range(0, unknowns, LANES):
            width = min(LANES, unknowns - q)
            blocks = [
                raw_ref[f * NODES + b * FACE + r + each, :, q : q + width]
                for each in range(2) for b in range(NODE1)
            ]
            both = jnp.concatenate(blocks, axis=0)
            high = both.astype(jnp.bfloat16)
            low = (both - high.astype(jnp.float32)).astype(jnp.bfloat16)
            if width == LANES:
                halves = jnp.concatenate([high, low], axis=1)
                out = lax.dot_general(eye_ref[...], halves, rows_of, preferred_element_type=jnp.float32)
            else:
                eye = eye_ref[:width, :width]
                out = lax.dot_general(eye, high, rows_of, preferred_element_type=jnp.float32)
                out = out + lax.dot_general(eye, low, rows_of, preferred_element_type=jnp.float32)
            for each in range(2):
                tt_ref[f * FACE + r + each, q : q + width, :] = out[:, each * LANES : (each + 1) * LANES]

    for part_of in range(len(LOADS)):
        load(part_of)

    row = lax.broadcasted_iota(jnp.int32, (SUB, LANES), 0)
    lane = lax.broadcasted_iota(jnp.int32, (SUB, LANES), 1)
    group = lane // count
    local = lane - group * count
    top = row < NODE1
    k_of = row % NODE1
    block = group[:1]

    def event(x, chunk):
        if x == 0:
            return 0
        return 1 + chunk + sum(len(chunks_of(each)) for each in range(1, min(x, 3)))

    def copies(x, chunk):
        first, fields = chunks_of(x)[chunk]
        rows = pl.ds(first * FACE, fields * FACE)
        zrows = pl.ds(chunk * SUB, SUB)
        out = []
        for which in range(4):
            if which < 2:
                src, dst = y_ref.at[x, rows], recv_ref.at[x, which, rows]
                target = at(1) if which == 0 else at(-1)
            else:
                src, dst = zsend_ref.at[x, zrows], zrecv_ref.at[x, which - 2, zrows]
                target = at(-rotation) if which == 2 else at(-rotation - 1)
            out.append(pltpu.make_async_remote_copy(
                src_ref=src, dst_ref=dst, send_sem=send_sem.at[which // 2],
                recv_sem=recv_sem.at[event(x, chunk)], device_id={"elem": target}, device_id_type=MESH,
            ))
        return out

    def arrived(xs, chunks):
        rows = sum(2 * chunks_of(xs[0])[chunk][1] * FACE + 2 * SUB for chunk in chunks) * len(xs)
        there = tt_ref.at[0, pl.ds(0, rows)]
        pltpu.make_async_copy(there, there, recv_sem.at[event(xs[0], chunks[0])]).wait()

    def packed_rows(values, k):
        packed = jnp.zeros((SUB, LANES), jnp.float32)
        for slot, value in enumerate(values):
            shift = (slot - k) % SUB
            value = pltpu.roll(value, shift, 0) if shift else value
            packed = jnp.where(k_of == slot, value, packed)
        return packed

    def chunk_rows(x, chunk):
        first, fields = chunks_of(x)[chunk]
        return [c_rows(first + slot // 2, slot % 2) for slot in range(2 * fields)]

    def send(x, chunk):
        packed = packed_rows([y_ref[x, rows, :] for rows in chunk_rows(x, chunk)], 0)
        zsend_ref[x, chunk * SUB : (chunk + 1) * SUB, :] = packed
        out = copies(x, chunk)
        for which in (0, 1, 3, 2):
            out[which].start()

    for each in small:
        each.wait()
    uc[...] = jnp.concatenate([u_ref[...]] * SECTIONS, axis=0).T
    for f in range(FIELDS):
        for half in range(2):
            value = uc[g_rows(f, NODE1 - 1, half), :]
            for i in range(NODE1 - 2, -1, -1):
                value = jnp.where(group == i, uc[g_rows(f, i, half), :], value)
            y_ref[0, c_rows(f, half), :] = value

    to_k_order(uc, uk)
    volume(uc, uk, lc, tk, 1.0)
    pl.semaphore_wait(barrier, len(others))
    for chunk in range(len(CHUNKS)):
        send(0, chunk)

    def found(wanted, offsets):
        index = wanted - at(offsets[0]) * count
        code = jnp.zeros_like(wanted)
        for at_code, offset in enumerate(offsets[1:]):
            here = wanted - at(offset) * count
            match = (here >= 0) & (here < count)
            index = jnp.where(match, here, index)
            code = jnp.where(match, at_code + 1, code)
        return index, code

    def beside(face):
        wanted = jnp.concatenate([nbr_ref[face : face + 1, :]] * SECTIONS, axis=1)
        return found(jnp.broadcast_to(wanted, (SUB, LANES)), (0, -1, 1))

    per_row = LANES // count
    listed = partner_ref[pl.ds(rank // per_row, 1), :]
    partner = jnp.zeros((1, LANES), jnp.int32)
    for index in range(per_row):
        part_row = jnp.concatenate([listed[:, index * count : (index + 1) * count]] * SECTIONS, axis=1)
        partner = jnp.where(rank % per_row == index, part_row, partner)
    faces = [beside(face) for face in range(5)]
    picks = [
        [
            jnp.where(group == 0, faces[0][0] + (NODE1 - 1) * count, faces[1][0]),
            jnp.where(group == 0, faces[0][1], faces[1][1]),
        ],
        [jnp.where(top, low, high) + shift for low, high, shift in zip(
            faces[2], faces[3], (group * count, 0))],
        [faces[4][0] + group * count, faces[4][1]],
    ]
    index, code = found(jnp.broadcast_to(partner, (SUB, LANES)), (rotation, rotation + 1))
    picks.append([index + group * count, code])
    for kind in range(4):
        for which in range(2):
            index_ref[kind, which] = picks[kind][which]
    def picked(kind, own, values):
        index = index_ref[kind, 0]
        code = index_ref[kind, 1]
        for at_code, value in enumerate(values):
            own = jnp.where(code == at_code + 1, take(value, index), own)
        return own

    def crossed(low, high):
        return pltpu.roll(jnp.where(top, low, high), NODE1, 0)

    def own_near(x, slot):
        for chunk, (first, fields) in enumerate(chunks_of(x)):
            for f in range(first, first + fields):
                low, high = [y_ref[x, c_rows(f, half), :] for half in range(2)]
                own_ref[slot, f, 0] = take(low, index_ref[0, 0])
                own_ref[slot, f, 1] = take(high, index_ref[0, 0])
                own_ref[slot, f, 2] = take(crossed(low, high), index_ref[1, 0])
            minus = packed_rows([y_ref[x, rows, :] for rows in chunk_rows(x, chunk)], NODE1 - 1)
            own_z[slot, chunk] = take(minus, index_ref[2, 0])

    own_near(0, 0)
    out_row = lax.broadcasted_iota(jnp.int32, eye_ref.shape, 0)
    out_lane = lax.broadcasted_iota(jnp.int32, eye_ref.shape, 1)
    eye_ref[...] = jnp.where(out_row == out_lane % LANES, 1.0, 0.0).astype(jnp.bfloat16)
    for f in range(FIELDS):
        loaded(f)
        for r in range(SPLIT_AT, FACE, 2):
            transposed_pair(f, r)
        for r in range(SPLIT_AT):
            transposed(f, r)

    def near_compact(x, slot, chunk):
        first, fields = chunks_of(x)[chunk]
        sides = []
        for f in range(first, first + fields):
            low, high = [
                [recv_ref[x, which, c_rows(f, half), :] for which in range(2)] for half in range(2)
            ]
            own = [own_ref[slot, f, each] for each in range(3)]
            y = picked(1, own[2], [crossed(a, b) for a, b in zip(low, high)])
            sides.append((picked(0, own[0], low), picked(0, own[1], high), y))
        there = chunk_rows(x, chunk)
        minus = [
            packed_rows([recv_ref[x, which, rows, :] for rows in there], NODE1 - 1) for which in range(2)
        ]
        plus = [zrecv_ref[x, which, chunk * SUB : (chunk + 1) * SUB, :] for which in range(2)]
        plus = picked(3, take(plus[0], index_ref[3, 0]), plus[1:])
        return sides, picked(2, own_z[slot, chunk], minus), plus

    def spread(value):
        turned = [value] + [pltpu.roll(value, i * count, 1) for i in range(1, NODE1)]
        out = []
        for i in range(NODE1):
            each = turned[(NODE1 - 1 - i) % NODE1]
            for c in range(NODE1 - 2, -1, -1):
                each = jnp.where(group == c, turned[(c - i) % NODE1], each)
            out.append(each)
        return out

    def z_state(minus, plus, slot):
        if slot:
            minus = pltpu.roll(minus, SUB - slot, 0)
        if slot != NODE1 - 1:
            plus = pltpu.roll(plus, NODE1 - 1 - slot, 0)
        return jnp.where(k_of == 0, minus, jnp.where(k_of == NODE1 - 1, plus, 0.0))

    def spread_near(x, chunk, near, put):
        sides, minus, plus = near
        minus, plus = spread(minus), spread(plus)
        first, fields = chunks_of(x)[chunk]
        for each, (x_low, x_high, y) in enumerate(sides):
            f = first + each
            for half, value in enumerate((x_low, x_high)):
                out = spread(value)
                for side, i in enumerate((0, NODE1 - 1)):
                    put(X_SLOT + 2 * side + half, f, out[i])
            out = spread(y)
            for i in range(NODE1):
                put(Y_SLOT + i, f, out[i])
                for half in range(2):
                    put(Z_SLOT + 2 * i + half, f, z_state(minus[i], plus[i], 2 * each + half))

    x_side = (group == 0) | (group == NODE1 - 1)

    def lift(x, chunk, near, v, scale=None):
        sides, minus, plus = near
        first, fields = chunks_of(x)[chunk]
        for each, (x_low, x_high, y) in enumerate(sides):
            for half, value in enumerate((x_low, x_high)):
                value = jnp.where(x_side, value, 0.0) + z_state(minus, plus, 2 * each + half)
                value = value + jnp.where(top if half == 0 else ~top, y, 0.0)
                if scale is not None:
                    value = scale * value
                out = spread(value)
                for i in range(NODE1):
                    x_ref[v, g_rows(first + each, i, half), :] = out[i]

    def folded(accs):
        for bit in (1, 2, 4):
            low = (row & bit) == 0
            accs = [
                jnp.where(low, a, pltpu.roll(b, bit, 0)) + jnp.where(low, pltpu.roll(a, SUB - bit, 0), b)
                for a, b in zip(accs[::2], accs[1::2])
            ]
        return accs[0]

    def product(t, xs, dst, fields, first, last):
        vectors = len(xs)
        accs = [[None] * SUB for _ in range(vectors)]
        if not first:
            accs = [[acc_ref[v, t, a] for a in range(SUB)] for v in range(vectors)]
        for q in range(fields[0] * SUB, (fields[0] + fields[1]) * SUB):
            rows = slice(q * SUB, (q + 1) * SUB)
            parts_of = [x[rows, :] for x in xs]
            for a in range(SUB):
                m = tt_ref[t * SUB + a, rows, :]
                for v in range(vectors):
                    term = m * parts_of[v]
                    accs[v][a] = term if accs[v][a] is None else accs[v][a] + term
        for v in range(vectors):
            if last:
                dst[v][t * SUB : (t + 1) * SUB, :] = folded(accs[v])
            else:
                for a in range(SUB):
                    acc_ref[v, t, a] = accs[v][a]

    blocks = FIELDS * FACE // SUB

    def whole(xs, dst, sends):
        for chunk, (first, fields) in enumerate(chunks_of(sends[0])):
            for t in range(2 * first, 2 * (first + fields)):
                product(t, xs, dst, (0, FIELDS), True, True)
            for x in sends:
                send(x, chunk)

    def by_chunk(source, xs, dst, sends, await_chunk, ready, finish=None, lead=0):
        await_chunk(0)
        ready(0)
        arriving = chunks_of(source)
        for chunk, fields in enumerate(arriving[:-1]):
            if chunk >= lead:
                await_chunk(chunk + 1)
                ready(chunk + 1)
            for t in range(blocks):
                product(t, xs, dst, fields, chunk == 0, False)
            if chunk < lead:
                await_chunk(chunk + 1)
                ready(chunk + 1)
        for chunk, (first, fields) in enumerate(chunks_of(sends[0]) if sends else FINE):
            for t in range(2 * first, 2 * (first + fields)):
                product(t, xs, dst, arriving[-1], False, True)
            for x in sends:
                send(x, chunk)
            if finish is not None:
                finish(chunk)

    def put_first(slot, f, value):
        near_ref[slot, f] = value

    every = range(len(CHUNKS))
    arrived([0], every)
    for chunk in every:
        spread_near(0, chunk, near_compact(0, 0, chunk), put_first)
    surface(uc, near_ref, lc, 1.0)
    whole([lc], [y_ref.at[1]], [1])
    own_near(1, 0)

    def ready_v(chunk):
        near = near_compact(1, 0, chunk)
        lift(1, chunk, near, 0)
        sides, minus, plus = near
        for each, side in enumerate(sides):
            for slot, value in enumerate(side):
                near_v[chunks_of(1)[chunk][0] + each, slot] = value
        near_z[chunk, 0] = minus
        near_z[chunk, 1] = plus

    by_chunk(1, [x_ref.at[0]], [y_ref.at[2]], [2], lambda chunk: arrived([1], [chunk]), ready_v)
    own_near(2, 0)

    def alpha(i):
        return time_step * sum(butcher[i])

    def coupling(i):
        return time_step * butcher[i][i] * dissipation * inv_weight

    def own(p, s):
        return p * own_sections + s % own_sections

    def per_part(value_of):
        value = jnp.float32(value_of(0))
        for other in range(1, parts):
            value = jnp.where(part == other, jnp.float32(value_of(other)), value)
        return value

    def per_lane(value_of):
        out = jnp.zeros((1, LANES), jnp.float32)
        for s in range(SECTIONS):
            out = jnp.where(block == s, per_part(lambda p, s=s: value_of(p, s)), out)
        return out

    alphas = per_lane(lambda p, s: alpha(s))
    betas = per_lane(lambda p, s: alpha(s) * coupling(s))

    for f in range(FIELDS):
        for half in range(2):
            v, w = y_ref[1, c_rows(f, half), :], y_ref[2, c_rows(f, half), :]
            for i, (v, w) in enumerate(zip(spread(v), spread(w))):
                rows = g_rows(f, i, half)
                vc[rows, :] = v
                wc[rows, :] = w
    gc[...] = uc[...] + alphas * vc[...] + betas * wc[...]
    to_k_order(gc, uk)
    volume(gc, uk, lc, tk, time_step)

    def add_v(slot, f, value):
        near_ref[slot, f] = near_ref[slot, f] + alphas * value

    def add_w(slot, f, value):
        near_ref[slot, f] = near_ref[slot, f] + betas * value

    for chunk, (first, fields) in enumerate(chunks_of(1)):
        sides = [[near_v[f, slot] for slot in range(3)] for f in range(first, first + fields)]
        spread_near(1, chunk, (sides, near_z[chunk, 0], near_z[chunk, 1]), add_v)
    sections = range(own_sections)
    own_alphas = [per_part(lambda p, s=s: alpha(own(p, s))) for s in sections]
    own_betas = [per_part(lambda p, s=s: alpha(own(p, s)) * coupling(own(p, s))) for s in sections]
    own_couplings = [per_part(lambda p, s=s: coupling(own(p, s))) for s in sections]
    weights = [
        [per_lane(lambda p, g, s=s, r=r: butcher[own(p, s)][(g - r) % SECTIONS]) for r in range(SECTIONS)]
        for s in sections
    ]
    for s in sections:
        x_ref[s] = -(own_alphas[s] * vc[...] + own_betas[s] * wc[...])
    for chunk in every:
        arrived([2], [chunk])
        spread_near(2, chunk, near_compact(2, 0, chunk), add_w)
    surface(gc, near_ref, lc, time_step)

    for start in range(0, unknowns, SUB):
        rows = slice(start, start + SUB)
        tend = lc[rows, :]
        turned = [tend] + [pltpu.roll(tend, r * count, 1) for r in range(1, SECTIONS)]
        for s in sections:
            total = x_ref[s, rows, :]
            for r in range(SECTIONS):
                total = total + weights[s][r] * turned[r]
            x_ref[s, rows, :] = total

    operands = [x_ref.at[s] for s in sections]
    whole(operands, [y_ref.at[3 + s] for s in sections], [3 + s for s in sections])

    def await_first(chunk):
        arrived([3 + s for s in sections], [chunk])

    def ready_first(chunk):
        for s in sections:
            lift(3 + s, chunk, near_compact(3 + s, s, chunk), s, own_couplings[s])

    for s in sections:
        own_near(3 + s, s)
    def kept(f, half, s):
        start = ((2 * s + half) * FIELDS + f) * SUB
        return slice(start, start + SUB)

    for f in range(FIELDS):
        for half in range(2):
            rows = c_rows(f, half)
            for s in sections:
                vc[kept(f, half, s), :] = (
                    own_alphas[s] * y_ref[1, rows, :]
                    + own_betas[s] * y_ref[2, rows, :]
                    + y_ref[3 + s, rows, :]
                )

    def finish(f):
        for half in range(2):
            values = [
                spread(vc[kept(f, half, s), :] + last_ref[s, c_rows(f, half), :]) for s in sections
            ]
            for i in range(NODE1):
                value = values[0][i]
                for s in sections[1:]:
                    value = jnp.where(group == s, values[s][i], value)
                gc[g_rows(f, i, half), :] = value
        if f % 2 or f == FIELDS - 1:
            first = f - f % 2
            columns = slice(first * NODES, (f + 1) * NODES)
            done = gc[columns, :].T
            for s in sections:
                out_ref[s, :, columns] = done[s * count : (s + 1) * count]

    by_chunk(3, operands, [last_ref.at[s] for s in sections], [], await_first, ready_first, finish, 2)

    sent = sum(len(chunks_of(x)) for x in range(3 + own_sections)) * 2 * SUB
    for which, there in enumerate((recv_ref, tt_ref.at[pl.ds(0, 2), pl.ds(0, sent // 2)])):
        pltpu.make_async_copy(there, there, send_sem.at[which]).wait()


def on_device(u_start, inverses, neighbours, partners):
    count, unknowns = u_start.shape
    devices = lax.axis_size("elem")
    own_sections = SECTIONS // lax.axis_size("section")
    listed = partners.reshape(-1, LANES)
    exchanges = 3 + own_sections
    column = pltpu.VMEM((unknowns, LANES), jnp.float32)
    compact = FIELDS * FACE
    packed = len(FINE) * SUB
    change = pl.pallas_call(
        functools.partial(kernel, devices, count),
        out_shape=pltpu.VMEM((own_sections, count, unknowns), jnp.float32),
        in_specs=[pl.BlockSpec(memory_space=pl.ANY)] * 4,
        out_specs=pl.BlockSpec(memory_space=pltpu.VMEM),
        scratch_shapes=[
            pltpu.VMEM(u_start.shape, jnp.float32),
            pltpu.VMEM(neighbours.shape[::-1], jnp.int32),
            pltpu.VMEM(listed.shape, jnp.int32),
            pltpu.VMEM((unknowns, count, unknowns), jnp.float32),
            pltpu.VMEM((compact, unknowns, LANES), jnp.float32),
            pltpu.VMEM((exchanges, compact, LANES), jnp.float32),
            pltpu.VMEM((exchanges, packed, LANES), jnp.float32),
            pltpu.VMEM((exchanges, 2, compact, LANES), jnp.float32),
            pltpu.VMEM((exchanges, 2, packed, LANES), jnp.float32),
            pltpu.VMEM((4, 2, SUB, LANES), jnp.int32),
            pltpu.VMEM((FIELDS, 3, SUB, LANES), jnp.float32),
            pltpu.VMEM((len(FINE), 2, SUB, LANES), jnp.float32),
            pltpu.VMEM((16, FIELDS, SUB, LANES), jnp.float32),
            pltpu.VMEM((own_sections, FIELDS, 3, SUB, LANES), jnp.float32),
            pltpu.VMEM((own_sections, len(FINE), SUB, LANES), jnp.float32),
        ]
        + [column] * 7
        + [
            pltpu.VMEM((own_sections, unknowns, LANES), jnp.float32),
            pltpu.VMEM((own_sections, compact // SUB, SUB, SUB, LANES), jnp.float32),
            pltpu.VMEM((own_sections, compact, LANES), jnp.float32),
            pltpu.VMEM((LANES, 2 * LANES), jnp.bfloat16),
            pltpu.SemaphoreType.DMA((3,)),
            pltpu.SemaphoreType.DMA((len(LOADS),)),
            pltpu.SemaphoreType.DMA((2,)),
            pltpu.SemaphoreType.DMA((1 + len(CHUNKS) + 2 * len(FINE),)),
        ],
        compiler_params=pltpu.CompilerParams(
            collective_id=0, has_side_effects=True, vmem_limit_bytes=VMEM_BYTES
        ),
    )(u_start, neighbours.T, listed, inverses)
    return u_start[None] + change


def solution(mesh):
    placed = (P("elem", None), P("elem", None, None), P("elem", None), P())
    return jax.shard_map(
        on_device, mesh=mesh, in_specs=placed, out_specs=P("section", "elem", None), check_vma=False
    )
```
